32 devices in a mesh: req: 2 (over y), tm: 4 (over z), rows: 2 (over x), sub: 2 (over core).
Axes of the slice: x: 2, y: 2, z: 4, core: 2. Of those that a mesh axis runs over, the one named last changes fastest.
Arguments:
- latents: bfloat16 [32, 256, 640], P('tm', ('req', 'rows')), parts along dimension 1, may hold values from -6 to 6
- cotangent: bfloat16 [32, 256, 640], P('tm', ('req', 'rows')), parts along dimension 1, may hold values from -6 to 6
- w_qkv: bfloat16 [640, 3, 640], P(None, None, 'sub'), may hold values from -0.25 to 0.25
- w_out: bfloat16 [640, 640], P('sub'), may hold values from -0.25 to 0.25
- time_bias: float32 [8, 63], replicated, may hold values from -4 to 310
Outputs:
- grad_latents: bfloat16 [32, 256, 640], P('tm', ('req', 'rows'), 'sub'), parts along dimension 1
- grad_w_qkv: float32 [1280, 3, 640], P(('req', 'tm', 'rows'), None, 'sub'), parts along dimension 0
- grad_w_out_t: float32 [1280, 640], P(('req', 'tm', 'rows'), 'sub'), parts along dimension 0
The draws below stay inside these ranges and needn't reach their ends.
There are 2 independent parts, one for each index of `req`. The reference program is written for one: setup_inputs(seed, part) draws one part's arguments, and reference() takes and returns one part's arrays. A program takes and returns all parts, laid end to end along the dimension named above; an argument that names none is the same for every part. Nothing has to cross between parts.
All inputs are finite; a program needn't handle non-finite values.
Results may differ from the reference program's by a relative error of at most 0.012.
Values may be sent and summed in bfloat16 or wider, within the bound.
No kernel may reach another device: no remote copies, remote signals or barrier semaphores. Data moves between devices by JAX's collectives and lax.ppermute only.
A program may use at most 128 MiB of HBM per device.

```python
import math
import jax
import jax.numpy as jnp
from jax import lax

C = 640
H = 8
F = 32
S = 128
N_SUB = 2


def draw_time_bias(key, part):
    values = jnp.clip(jax.random.normal(key, (H, 2 * F - 1), jnp.float32), -4.0, 4.0)
    return values


def spiked(entries, stream_key, source, target, blocks, factor):
    owner, partner = [(jnp.arange(entries.shape[axis_at]) // (entries.shape[axis_at] // blocks)).reshape([-1 if axis == axis_at else 1 for axis in range(entries.ndim)]) for axis_at in (source, target)]
    chosen = jax.random.permutation(stream_key, blocks)[partner]
    strong = (owner == chosen) | (owner == (partner + blocks // 2) % blocks)
    return jnp.where(strong, factor * entries, entries)


def levels(stream_key, dims, split, least, largest):
    level, own = 1.0, jax.random.fold_in(stream_key, 6)
    for axis_at, shards_of in split:
        heights = jnp.exp(jax.random.uniform(jax.random.fold_in(own, axis_at), (shards_of,), jnp.float32, least / len(split), largest / len(split)))
        level = level * jnp.repeat(heights, dims[axis_at] // shards_of).reshape([-1 if axis == axis_at else 1 for axis in range(len(dims))])
    return level


def bell_draw(rng, dims, spread, limit, shards=(), kind=jnp.bfloat16):
    result = spread * jax.random.normal(rng, dims, jnp.float32)
    if shards:
        result = result * levels(rng, dims, shards, -0.22, 0.18)
    return jnp.clip(result, -limit, limit).astype(kind)


def gaussian_with(stream_key, extent, scale, reach, cuts, heavy, kind=jnp.bfloat16):
    entries = scale * jax.random.normal(stream_key, extent, jnp.float32)
    if cuts:
        entries = entries * levels(stream_key, extent, cuts, -0.22, 0.18)
    return jnp.clip(spiked(entries, jax.random.fold_in(stream_key, 3), *heavy), -reach, reach).astype(kind)


def setup_inputs(seed: int = 0, part: int = 0) -> dict:
    key_of = jax.random.split(jax.random.key(seed), 6)
    part_splits = jax.random.split(jax.random.fold_in(key_of[5], part), 6)
    latents = gaussian_with(part_splits[0], (F, S, C), 1.0, 6.0, ((0, 4), (1, 2)), (0, 2, 4, 2.0))
    cotangent = gaussian_with(part_splits[1], (F, S, C), 1.0, 6.0, ((0, 4), (1, 2)), (1, 2, 2, 2.0))
    w_qkv = bell_draw(key_of[2], (C, 3, C), C ** -0.5, 0.25, ((2, 2),))
    w_out = bell_draw(key_of[3], (C, C), C ** -0.5, 0.25, ((0, 2),))
    time_bias = draw_time_bias(jax.random.fold_in(key_of[5], 71), part)
    return dict(latents=latents, cotangent=cotangent, w_qkv=w_qkv, w_out=w_out, time_bias=time_bias)


def positional(frame_pos, channels):
    half = channels // 2
    frequency = jnp.exp(-math.log(10000.0) * jnp.arange(half, dtype=jnp.float32) * 2.0 / channels)
    angles = frame_pos.astype(jnp.float32)[:, None] * frequency[None, :]
    return jnp.concatenate((jnp.sin(angles), jnp.cos(angles)), axis=1)

def bias_table(bias_rows, frames):
    offsets = jnp.arange(frames, dtype=jnp.int32)[:, None] - jnp.arange(frames, dtype=jnp.int32)[None, :] + frames - 1
    return bias_rows[:, offsets]

def reference(latents, cotangent, w_qkv, w_out, time_bias):
    frames, positions, channels = latents.shape
    head_size = channels // H
    inv_root = 1.0 / math.sqrt(head_size)
    hidden = (latents.astype(jnp.float32) + positional(jnp.arange(frames, dtype=jnp.int32), channels)[:, None, :]).astype(jnp.bfloat16)
    qkv = jnp.einsum('fsc,ctd->fstd', hidden.astype(jnp.float32), w_qkv.astype(jnp.float32)).astype(jnp.bfloat16)
    grad_attn = jnp.einsum('fse,de->fsd', cotangent.astype(jnp.float32), w_out.astype(jnp.float32)).astype(jnp.bfloat16)
    bias_full = bias_table(time_bias, frames)

    def per_position(items):
        query_rows, key_rows, value_rows, grad_rows = items
        shape3 = (frames, H, head_size)
        query_heads = query_rows.reshape(shape3).astype(jnp.float32)
        key_heads = key_rows.reshape(shape3).astype(jnp.float32)
        value_heads = value_rows.reshape(shape3).astype(jnp.float32)
        grad_heads = grad_rows.reshape(shape3).astype(jnp.float32)
        scores = jnp.einsum('ihd,jhd->hij', query_heads, key_heads) * inv_root + bias_full
        row_max = lax.optimization_barrier(jnp.max(scores, axis=-1, keepdims=True))
        raw_weights = jnp.exp(scores - row_max)
        probs = raw_weights / lax.optimization_barrier(jnp.sum(raw_weights, axis=-1, keepdims=True))
        probs_low = probs.astype(jnp.bfloat16).astype(jnp.float32)
        attn_out = jnp.einsum('hij,jhd->ihd', probs_low, value_heads).astype(jnp.bfloat16)
        grad_probs = jnp.einsum('ihd,jhd->hij', grad_heads, value_heads)
        row_dot = lax.optimization_barrier(jnp.sum(probs * grad_probs, axis=-1, keepdims=True))
        grad_scores = (probs * (grad_probs - row_dot) * inv_root).astype(jnp.bfloat16).astype(jnp.float32)
        grad_query = jnp.einsum('hij,jhd->ihd', grad_scores, key_heads).astype(jnp.bfloat16)
        grad_key = jnp.einsum('hij,ihd->jhd', grad_scores, query_heads).astype(jnp.bfloat16)
        grad_value = jnp.einsum('hij,ihd->jhd', probs_low, grad_heads).astype(jnp.bfloat16)
        flat = (frames, channels)
        return (attn_out.reshape(flat), grad_query.reshape(flat), grad_key.reshape(flat), grad_value.reshape(flat))
    moved = (jnp.transpose(qkv[:, :, 0], (1, 0, 2)), jnp.transpose(qkv[:, :, 1], (1, 0, 2)), jnp.transpose(qkv[:, :, 2], (1, 0, 2)), jnp.transpose(grad_attn, (1, 0, 2)))
    attn_out, grad_query, grad_key, grad_value = lax.map(per_position, moved)
    attn_out = jnp.transpose(attn_out, (1, 0, 2))
    grad_qkv = jnp.stack((jnp.transpose(grad_query, (1, 0, 2)), jnp.transpose(grad_key, (1, 0, 2)), jnp.transpose(grad_value, (1, 0, 2))), axis=2)
    grad_w_qkv = jnp.einsum('fsc,fstd->ctd', hidden.astype(jnp.float32), grad_qkv.astype(jnp.float32))
    grad_w_out_t = jnp.einsum('fse,fsd->ed', cotangent.astype(jnp.float32), attn_out.astype(jnp.float32))
    group_width = channels // N_SUB
    summed_back = jnp.zeros((frames, positions, channels), jnp.float32)
    for head_group in range(N_SUB):
        lower = head_group * group_width
        term = jnp.einsum('fstd,ctd->fsc', grad_qkv[..., lower:lower + group_width].astype(jnp.float32), w_qkv[..., lower:lower + group_width].astype(jnp.float32)).astype(jnp.bfloat16)
        term = lax.optimization_barrier(term)
        summed_back = summed_back + term.astype(jnp.float32)
    grad_latents = (cotangent.astype(jnp.float32) + summed_back).astype(jnp.bfloat16)
    return (grad_latents, grad_w_qkv, grad_w_out_t)
```

```python
import functools
import math

import jax
import jax.numpy as jnp
from jax import lax
from jax.experimental import pallas as pl
from jax.experimental.pallas import tpu as pltpu
from jax.sharding import PartitionSpec as P

H = 8
VMEM = pl.BlockSpec(memory_space=pltpu.VMEM)
ANY = pl.BlockSpec(memory_space=pl.ANY)
BF16 = jnp.bfloat16
F32 = jnp.float32


def params():
    return pltpu.CompilerParams(vmem_limit_bytes=48 << 20)


def shift_send(array, axis, step):
    size = lax.axis_size(axis)
    return lax.ppermute(array, axis, [(i, (i + step) % size) for i in range(size)])


def dot_nn(a, b):
    return lax.dot_general(a, b, (((1,), (0,)), ((), ())), preferred_element_type=F32)


def dot_nt(a, b):
    return lax.dot_general(a, b, (((1,), (1,)), ((), ())), preferred_element_type=F32)


def dot_tn(a, b):
    return lax.dot_general(a, b, (((0,), (0,)), ((), ())), preferred_element_type=F32)


def positional(frames, channels):
    half = channels // 2
    frequency = jnp.exp(-math.log(10000.0) * jnp.arange(half, dtype=F32) * 2.0 / channels)
    angles = jnp.arange(frames, dtype=jnp.int32).astype(F32)[:, None] * frequency[None, :]
    return jnp.concatenate((jnp.sin(angles), jnp.cos(angles)), axis=1)


def split_kernel(count, width, lat_ref, cot_ref, own_lat, own_cot, *rest):
    sends, sems = rest[: count - 1], rest[count - 1]
    me = lax.axis_index("tm")
    core = lax.axis_index("sub")

    def block(ref, step):
        start = pl.multiple_of(lax.rem(me + step, count) * width, width)
        return ref.at[:, pl.ds(start, width), :]

    def move(ref):
        copies = [
            pltpu.make_async_copy(block(ref, step), sends[step - 1], sems.at[step + 1])
            for step in range(1, count)
        ]
        for copy in copies:
            copy.start()
        for copy in copies:
            copy.wait()

    own = [
        pltpu.make_async_copy(block(lat_ref, 0), own_lat, sems.at[0]),
        pltpu.make_async_copy(block(cot_ref, 0), own_cot, sems.at[1]),
    ]

    @pl.when(core == 0)
    def _():
        move(lat_ref)

    @pl.when(core != 0)
    def _():
        move(cot_ref)

    for copy in own:
        copy.start()
    for copy in own:
        copy.wait()


def split_rows(latents, cotangent, count):
    frames, positions, channels = latents.shape
    width = positions // count
    if width % 16 == 0:
        shape = jax.ShapeDtypeStruct((frames, width, channels), BF16)
        blocks = pl.pallas_call(
            functools.partial(split_kernel, count, width),
            out_shape=[shape] * (count + 1),
            in_specs=[ANY] * 2,
            out_specs=[ANY] * (count + 1),
            scratch_shapes=[pltpu.SemaphoreType.DMA((count + 1,))],
            compiler_params=params(),
            name="split_rows",
        )(latents, cotangent)
    else:
        me = lax.axis_index("tm")
        sent = jnp.where(lax.axis_index("sub") == 0, latents, cotangent)

        def cut(array, step):
            start = lax.rem(me + step, count) * width
            return lax.dynamic_slice_in_dim(array, start, width, 1)

        blocks = [cut(latents, 0), cut(cotangent, 0)] + [cut(sent, k) for k in range(1, count)]
    blocks = [b.reshape(frames * width, channels) for b in blocks]
    return blocks[0], blocks[1], blocks[2:]


def table_kernel(frames, owners, width, bias_ref, table_ref, order_ref):
    heads = bias_ref.shape[0]
    group = table_ref.shape[0]
    lanes = bias_ref.shape[1]
    row = lax.broadcasted_iota(jnp.int32, (group, group), 0)
    col = lax.broadcasted_iota(jnp.int32, (group, group), 1)
    same = lax.div(row, frames) == lax.div(col, frames)
    for h in range(heads):
        spread = jnp.broadcast_to(bias_ref[h : h + 1, :], (group, lanes))
        skewed = pltpu.roll(spread, (1 - frames) % lanes, 1, stride=1, stride_axis=0)
        table_ref[:, h * group : (h + 1) * group] = jnp.where(same, skewed[:, :group], -1e30)
    rows = order_ref.shape[1]
    span = frames // owners

    def source(index):
        place, frame = lax.div(index, frames), lax.rem(index, frames)
        return lax.div(frame, span) * (span * width) + lax.rem(frame, span) * width + place

    here = lax.broadcasted_iota(jnp.int32, (rows, rows), 1)
    there = source(lax.broadcasted_iota(jnp.int32, (rows, 1), 0))
    order_ref[0] = jnp.where(here == there, 1.0, 0.0).astype(BF16)
    here = lax.broadcasted_iota(jnp.int32, (rows, rows), 0)
    there = source(lax.broadcasted_iota(jnp.int32, (1, rows), 1))
    order_ref[1] = jnp.where(here == there, 1.0, 0.0).astype(BF16)


def tables(time_bias, heads, frames, owners, width, group):
    first = lax.axis_index("sub") * heads
    own = jnp.flip(lax.dynamic_slice_in_dim(time_bias, first, heads, 0), 1)
    lanes = -(-max(2 * frames - 1, group) // 128) * 128
    own = jnp.pad(own, ((0, 0), (0, lanes - own.shape[1])))
    rows = frames * width
    return pl.pallas_call(
        functools.partial(table_kernel, frames, owners, width),
        out_shape=[
            jax.ShapeDtypeStruct((group, heads * group), F32),
            jax.ShapeDtypeStruct((2, rows, rows), BF16),
        ],
        in_specs=[VMEM],
        out_specs=[VMEM] * 2,
        compiler_params=params(),
        name="tables",
    )(own)


def main_kernel(frames, owners, sides, block, heads, *refs):
    parts = 2 * owners
    inputs, refs = refs[:parts], refs[parts:]
    pe_ref, table_ref, order_ref, w_qkv_ref, w_out_ref = refs[:5]
    refs = refs[5:]
    split = block % 16 == 0
    weight_outs = 2 * sides if split else 2
    weight_refs, refs = refs[:weight_outs], refs[weight_outs:]
    back_keep, back_send, refs = refs[0], refs[1], refs[2:]
    rows_ref, hidden_ref, cot_ref, q_ref, k_ref, v_ref, g_ref, dqk_ref, dvo_ref, sems = refs

    me = lax.axis_index("tm")
    core = lax.axis_index("sub")
    side = lax.axis_index("rows")
    rows, channels = hidden_ref.shape
    width = q_ref.shape[1]
    size = width // heads
    group = table_ref.shape[0]
    inv_root = 1.0 / math.sqrt(size)

    copies = []
    for step in range(owners):
        owner = lax.rem(me - step + owners, owners)
        for which in range(2):
            kind = which if step == 0 else (core if which == 0 else 1 - core)
            copies.append(
                pltpu.make_async_copy(
                    inputs[2 * step + which], rows_ref.at[kind, owner], sems.at[2 * step + which]
                )
            )
    for copy in copies:
        copy.start()
    for copy in copies:
        copy.wait()

    order = order_ref[0]
    moved = dot_nn(order, rows_ref[0].reshape(rows, channels))
    pe = pe_ref[...]
    for start in range(0, rows, frames):
        hidden_ref[start : start + frames, :] = (moved[start : start + frames, :] + pe).astype(BF16)
    cot_ref[...] = dot_nn(order, rows_ref[1].reshape(rows, channels)).astype(BF16)

    hidden = hidden_ref[...]
    for t, ref in enumerate((q_ref, k_ref, v_ref)):
        ref[...] = dot_nt(hidden, w_qkv_ref[t]).astype(BF16)
    g_ref[...] = dot_nt(cot_ref[...], w_out_ref[...]).astype(BF16)

    lane = lax.broadcasted_iota(jnp.int32, (group, width), 1)
    masks = [(lane >= h * size) & (lane < (h + 1) * size) for h in range(heads)]
    zero = jnp.zeros((group, width), BF16)

    def stack(value):
        return jnp.concatenate([jnp.where(mask, value, zero) for mask in masks], axis=0)

    def flip(value):
        return jnp.concatenate(
            [value[:, h * group : (h + 1) * group].T for h in range(heads)], axis=1
        )

    for start in range(0, rows, group):
        span = slice(start, start + group)
        query, key, value, grad = q_ref[span, :], k_ref[span, :], v_ref[span, :], g_ref[span, :]
        keys, values = stack(key), stack(value)
        scores = dot_nt(query, keys) * inv_root + table_ref[...]
        grad_probs = dot_nt(grad, values)
        low, grad_scores = [], []
        for h in range(heads):
            part = slice(h * group, (h + 1) * group)
            own = scores[:, part]
            raw = jnp.exp(own - jnp.max(own, axis=1, keepdims=True))
            probs = raw / jnp.sum(raw, axis=1, keepdims=True)
            up = grad_probs[:, part]
            row_dot = jnp.sum(probs * up, axis=1, keepdims=True)
            low.append(probs.astype(BF16))
            grad_scores.append((probs * (up - row_dot) * inv_root).astype(BF16))
        low = jnp.concatenate(low, axis=1)
        grad_scores = jnp.concatenate(grad_scores, axis=1)
        attn_out = dot_nn(low, values)
        grad_query = dot_nn(grad_scores, keys)
        grad_key = dot_nn(flip(grad_scores), stack(query))
        grad_value = dot_nn(flip(low), stack(grad))
        dqk_ref[span, :] = jnp.concatenate([grad_query, grad_key], axis=1).astype(BF16)
        dvo_ref[span, :] = jnp.concatenate([grad_value, attn_out], axis=1).astype(BF16)

    def store(full, refs):
        if not split:
            refs[0][...] = full
            return
        for z in range(owners):
            slot = lax.rem(z - me + owners, owners)
            for x in range(sides):
                first = (z * sides + x) * block
                piece = full[first : first + block, :]
                turn = lax.rem(x - side + sides, sides)
                for j in range(sides):

                    @pl.when(turn == j)
                    def _(piece=piece, j=j, slot=slot):
                        refs[j][slot] = piece if j == 0 else piece.astype(BF16)

    half = len(weight_refs) // 2
    grad_vo = dvo_ref[...]
    grad_v, attn_out = grad_vo[:, :width], grad_vo[:, width:]
    store(
        jnp.concatenate([dot_tn(hidden, grad_v), dot_tn(cot_ref[...], attn_out)], axis=1),
        weight_refs[:half],
    )
    grad_qk = dqk_ref[...]
    store(dot_tn(hidden, grad_qk), weight_refs[half:])

    back = (
        dot_nn(grad_qk[:, :width], w_qkv_ref[0])
        + dot_nn(grad_qk[:, width:], w_qkv_ref[1])
        + dot_nn(grad_v, w_qkv_ref[2])
    ).astype(BF16)
    back = dot_nn(order_ref[1], back)
    chunk = rows // owners
    lower, upper = back[:, :width], back[:, width:]
    cot = rows_ref[1].reshape(rows, channels).astype(F32)

    def store_back(own, other, base):
        for z in range(owners):
            slot = lax.rem(z - me + owners, owners)
            span = slice(z * chunk, (z + 1) * chunk)
            back_keep[slot] = own[span, :] + base[span, :]
            back_send[slot] = other[span, :].astype(BF16)

    @pl.when(core == 0)
    def _():
        store_back(lower, upper, cot[:, :width])

    @pl.when(core != 0)
    def _():
        store_back(upper, lower, cot[:, width:])


def attend(inputs, pe, table, order, w_qkv, w_out, frames, owners, sides, heads):
    chunk, channels = inputs[0].shape
    rows = chunk * owners
    width = w_qkv.shape[1]
    block = channels // (owners * sides)
    if block % 16 == 0:
        keep = jax.ShapeDtypeStruct((owners, block, 2 * width), F32)
        send = jax.ShapeDtypeStruct((owners, block, 2 * width), BF16)
        weight_outs = ([keep] + [send] * (sides - 1)) * 2
    else:
        weight_outs = [jax.ShapeDtypeStruct((channels, 2 * width), F32)] * 2
    outs = weight_outs + [
        jax.ShapeDtypeStruct((owners, chunk, width), F32),
        jax.ShapeDtypeStruct((owners, chunk, width), BF16),
    ]
    result = pl.pallas_call(
        functools.partial(main_kernel, frames, owners, sides, block, heads),
        out_shape=outs,
        in_specs=[ANY] * len(inputs) + [VMEM] * 5,
        out_specs=[VMEM] * len(outs),
        scratch_shapes=[
            pltpu.VMEM((2, owners, chunk, channels), BF16),
            pltpu.VMEM((rows, channels), BF16),
            pltpu.VMEM((rows, channels), BF16),
            pltpu.VMEM((rows, width), BF16),
            pltpu.VMEM((rows, width), BF16),
            pltpu.VMEM((rows, width), BF16),
            pltpu.VMEM((rows, width), BF16),
            pltpu.VMEM((rows, 2 * width), BF16),
            pltpu.VMEM((rows, 2 * width), BF16),
            pltpu.SemaphoreType.DMA((2 * owners,)),
        ],
        compiler_params=params(),
        name="attend",
    )(*inputs, pe, table, order, w_qkv, w_out)
    back_keep, back_send = result[-2:]
    weights = []
    for at in range(2):
        if block % 16 == 0:
            part = result[at * sides : (at + 1) * sides]
            weights.append((part[0], list(part[1:])))
        else:
            full = result[at].reshape(owners, sides, block, 2 * width)
            full = jnp.roll(full, (-lax.axis_index("tm"), -lax.axis_index("rows")), (0, 1))
            weights.append((full[:, 0], [full[:, j].astype(BF16) for j in range(1, sides)]))
    return weights, back_keep, back_send


def combine_kernel(keep_ref, *refs):
    owners = keep_ref.shape[0]
    arrived, outs = refs[: len(refs) - owners], refs[len(refs) - owners :]
    for slot in range(owners):
        total = keep_ref[slot]
        for ref in arrived:
            total = total + ref[slot].astype(F32)
        outs[slot][...] = total.astype(outs[slot].dtype)


def combine(keep, arrived, own_dtype):
    owners = keep.shape[0]
    outs = [jax.ShapeDtypeStruct(keep.shape[1:], own_dtype)]
    outs += [jax.ShapeDtypeStruct(keep.shape[1:], BF16)] * (owners - 1)
    result = pl.pallas_call(
        combine_kernel,
        out_shape=outs,
        in_specs=[VMEM] * (1 + len(arrived)),
        out_specs=[VMEM] * owners,
        compiler_params=params(),
        name="combine",
    )(keep, *arrived)
    return result[0], result[1:]


def finish_kernel(count, *refs):
    ins, (w_qkv_ref, w_out_ref) = refs[:-2], refs[-2:]

    def total(parts):
        value = parts[0][...]
        for ref in parts[1:]:
            value = value + ref[...].astype(F32)
        return value

    width = w_out_ref.shape[1]
    value_out, query_key = total(ins[:count]), total(ins[count:])
    w_qkv_ref[0] = query_key[:, :width]
    w_qkv_ref[1] = query_key[:, width:]
    w_qkv_ref[2] = value_out[:, :width]
    w_out_ref[...] = value_out[:, width:]


def finish(value_out, query_key):
    block, width = value_out[0].shape[0], value_out[0].shape[1] // 2
    count = len(value_out)
    w_qkv, w_out = pl.pallas_call(
        functools.partial(finish_kernel, count),
        out_shape=[
            jax.ShapeDtypeStruct((3, block, width), F32),
            jax.ShapeDtypeStruct((block, width), F32),
        ],
        in_specs=[VMEM] * (2 * count),
        out_specs=[VMEM] * 2,
        compiler_params=params(),
        name="finish",
    )(*value_out, *query_key)
    return jnp.transpose(w_qkv, (1, 0, 2)), w_out


def place_kernel(*refs):
    blocks, out_ref, sems = refs[:-2], refs[-2], refs[-1]
    count, width = len(blocks), blocks[0].shape[1]
    me = lax.axis_index("tm")
    copies = []
    for step, ref in enumerate(blocks):
        start = pl.multiple_of(lax.rem(me - step + count, count) * width, width)
        copies.append(
            pltpu.make_async_copy(ref, out_ref.at[:, pl.ds(start, width), :], sems.at[step])
        )
    for copy in copies:
        copy.start()
    for copy in copies:
        copy.wait()


def place(blocks, frames):
    count = len(blocks)
    chunk, channels = blocks[0].shape
    width = chunk // frames
    blocks = [b.reshape(frames, width, channels) for b in blocks]
    if width % 16 == 0:
        return pl.pallas_call(
            place_kernel,
            out_shape=jax.ShapeDtypeStruct((frames, count * width, channels), BF16),
            in_specs=[ANY] * count,
            out_specs=ANY,
            scratch_shapes=[pltpu.SemaphoreType.DMA((count,))],
            compiler_params=params(),
            name="place",
        )(*blocks)
    me = lax.axis_index("tm")
    ordered = jnp.roll(jnp.stack(blocks[::-1]), me + 1, 0)
    return jnp.transpose(ordered, (1, 0, 2, 3)).reshape(frames, count * width, channels)


def per_device(latents, cotangent, w_qkv, w_out, time_bias):
    own_frames, positions, channels = latents.shape
    owners, sides = lax.axis_size("tm"), lax.axis_size("rows")
    frames = own_frames * owners
    heads = H // lax.axis_size("sub")
    width = positions // owners
    group = max(frames, 128)

    own_lat, own_cot, sends = split_rows(latents, cotangent, owners)
    table, order = tables(time_bias, heads, frames, owners, width, group)
    pe = positional(frames, channels)
    inputs = [own_lat, own_cot]
    for step, block in enumerate(sends):
        mine = shift_send(block, "tm", step + 1)
        inputs += [mine, shift_send(mine, "sub", 1)]
    weights, back_keep, back_send = attend(
        inputs,
        pe,
        table,
        order,
        jnp.transpose(w_qkv, (1, 2, 0)),
        w_out,
        frames,
        owners,
        sides,
        heads,
    )

    own_back, back_blocks = combine(back_keep, [shift_send(back_send, "sub", 1)], BF16)
    back_blocks = [own_back] + [
        shift_send(block, "tm", step + 1) for step, block in enumerate(back_blocks)
    ]
    sums = []
    for keep, side_blocks in weights:
        arrived = [shift_send(b, "rows", j + 1) for j, b in enumerate(side_blocks)]
        own, blocks = combine(keep, arrived, F32)
        sums.append([own] + [shift_send(b, "tm", step + 1) for step, b in enumerate(blocks)])
    grad_w_qkv, grad_w_out_t = finish(*sums)
    return (place(back_blocks, own_frames), grad_w_qkv, grad_w_out_t)


def solution(mesh):
    return jax.shard_map(
        per_device,
        mesh=mesh,
        in_specs=(
            P("tm", ("req", "rows"), None),
            P("tm", ("req", "rows"), None),
            P(None, None, "sub"),
            P("sub", None),
            P(),
        ),
        out_specs=(
            P("tm", ("req", "rows"), "sub"),
            P(("req", "tm", "rows"), None, "sub"),
            P(("req", "tm", "rows"), "sub"),
        ),
        check_vma=False,
    )
```

```python
import functools
import math

import jax
import jax.numpy as jnp
from jax import lax
from jax.experimental import pallas as pl
from jax.experimental.pallas import tpu as pltpu
from jax.sharding import PartitionSpec as P

H = 8
VMEM = pl.BlockSpec(memory_space=pltpu.VMEM)
HBM = pl.BlockSpec(memory_space=pltpu.HBM)
BF16 = jnp.bfloat16
F32 = jnp.float32


def params(limit=48 << 20):
    return pltpu.CompilerParams(vmem_limit_bytes=limit)


def shift_send(array, axis, step):
    size = lax.axis_size(axis)
    return lax.ppermute(array, axis, [(i, (i + step) % size) for i in range(size)])


def dot_nn(a, b):
    return lax.dot_general(a, b, (((1,), (0,)), ((), ())), preferred_element_type=F32)


def dot_nt(a, b):
    return lax.dot_general(a, b, (((1,), (1,)), ((), ())), preferred_element_type=F32)


def dot_tn(a, b):
    return lax.dot_general(a, b, (((0,), (0,)), ((), ())), preferred_element_type=F32)


def positional(frame_pos, channels):
    half = channels // 2
    frequency = jnp.exp(-math.log(10000.0) * jnp.arange(half, dtype=F32) * 2.0 / channels)
    angles = frame_pos.astype(F32)[:, None] * frequency[None, :]
    return jnp.concatenate((jnp.sin(angles), jnp.cos(angles)), axis=1)


def by_position(frames, width, back=False):
    rows = frames * width
    inner = width if back else frames
    outer = rows // inner
    row = lax.broadcasted_iota(jnp.int32, (rows, 1), 0)
    col = lax.broadcasted_iota(jnp.int32, (rows, rows), 1)
    source = lax.rem(row, inner) * outer + lax.div(row, inner)
    return jnp.where(col == source, 1.0, 0.0).astype(BF16)


def fetch(ref, owner, width, into, sem):
    start = pl.multiple_of(owner * width, width)
    return [
        pltpu.make_async_copy(ref.at[f, pl.ds(start, width), :], into.at[f], sem)
        for f in range(into.shape[0])
    ]


def block_of(ref, owner, width):
    return ref.at[:, pl.ds(pl.multiple_of(owner * width, width), width), :]


def turned(order, rows):
    frames, width, channels = rows.shape
    return dot_nn(order, rows.reshape(frames * width, channels)).astype(BF16)


def send_kernel(count, width, lat_ref, cot_ref, *refs):
    sends, rows_ref, sems = refs[: count - 1], refs[count - 1], refs[count]
    me = lax.axis_index("tm")
    core = lax.axis_index("sub")

    def copies(ref):
        return [
            pltpu.make_async_copy(
                block_of(ref, lax.rem(me + step, count), width),
                rows_ref.at[step - 1],
                sems.at[step - 1],
            )
            for step in range(1, count)
        ]

    def move(ref):
        moves = copies(ref)
        for copy in moves:
            copy.start()
        order = by_position(rows_ref.shape[1], width)
        for step, copy in enumerate(moves):
            copy.wait()
            sends[step][...] = turned(order, rows_ref[step])

    @pl.when(core == 0)
    def _():
        move(lat_ref)

    @pl.when(core != 0)
    def _():
        move(cot_ref)


def table_kernel(frames, owners, bias_ref, lat_ref, cot_ref, table_ref, own_lat, own_cot, *scratch):
    heads, lanes = bias_ref.shape
    group = table_ref.shape[0]
    span = frames // owners
    me = lax.axis_index("tm")
    copies = []
    if scratch:
        rows_ref, sems = scratch
        width = rows_ref.shape[2]
        for at, ref in enumerate((lat_ref, cot_ref)):
            copies.append(
                pltpu.make_async_copy(block_of(ref, me, width), rows_ref.at[at], sems.at[at])
            )
            copies[-1].start()

    def place_of(index):
        return lax.rem(lax.div(index, span), group // frames)

    def frame_of(index):
        owner = lax.rem(me - lax.div(index, group // owners) + owners, owners)
        return owner * span + lax.rem(index, span)

    row = lax.broadcasted_iota(jnp.int32, (group, 1), 0)
    col = lax.broadcasted_iota(jnp.int32, (1, group), 1)
    same = place_of(row) == place_of(col)
    left = jnp.where(frame_of(row) == col, 1.0, 0.0)
    right = jnp.where(row == frame_of(col), 1.0, 0.0)

    def exact(a, b):
        return lax.dot_general(
            a, b, (((1,), (0,)), ((), ())), precision=lax.Precision.HIGHEST,
            preferred_element_type=F32,
        )

    for h in range(heads):
        spread = jnp.broadcast_to(bias_ref[h : h + 1, :], (group, lanes))
        skewed = pltpu.roll(spread, (1 - frames) % lanes, 1, stride=1, stride_axis=0)
        turned_bias = exact(left, exact(skewed[:, :group], right))
        table_ref[:, h * group : (h + 1) * group] = jnp.where(same, turned_bias, -1e30)
    if scratch:
        order = by_position(span, width)
        for at, ref in enumerate((own_lat, own_cot)):
            copies[at].wait()
            ref[...] = turned(order, rows_ref[at])
    else:
        own_lat[...] = lat_ref[...]
        own_cot[...] = cot_ref[...]


def send_blocks(latents, cotangent, count):
    frames, positions, channels = latents.shape
    width = positions // count
    if width % 16 == 0:
        shape = jax.ShapeDtypeStruct((frames * width, channels), BF16)
        return pl.pallas_call(
            functools.partial(send_kernel, count, width),
            out_shape=[shape] * (count - 1),
            in_specs=[HBM] * 2,
            out_specs=[VMEM] * (count - 1),
            scratch_shapes=[
                pltpu.VMEM((count - 1, frames, width, channels), BF16),
                pltpu.SemaphoreType.DMA((count - 1,)),
            ],
            compiler_params=params(60 << 20),
            name="send_blocks",
        )(latents, cotangent)
    me = lax.axis_index("tm")
    sent = jnp.where(lax.axis_index("sub") == 0, latents, cotangent)
    return [cut(sent, lax.rem(me + step, count), width) for step in range(1, count)]


def cut(array, owner, width):
    block = lax.dynamic_slice_in_dim(array, owner * width, width, 1)
    return jnp.swapaxes(block, 0, 1).reshape(-1, array.shape[2])


def tables(time_bias, latents, cotangent, heads, owners, group):
    span, positions, channels = latents.shape
    frames, width = span * owners, positions // owners
    first = lax.axis_index("sub") * heads
    own = jnp.flip(lax.dynamic_slice_in_dim(time_bias, first, heads, 0), 1)
    lanes = -(-max(2 * frames - 1, group) // 128) * 128
    own = jnp.pad(own, ((0, 0), (0, lanes - own.shape[1])))
    scratch, specs = [], [VMEM] * 3
    if width % 16 == 0:
        scratch = [pltpu.VMEM((2, span, width, channels), BF16), pltpu.SemaphoreType.DMA((2,))]
        specs = [VMEM, HBM, HBM]
    else:
        me = lax.axis_index("tm")
        latents, cotangent = cut(latents, me, width), cut(cotangent, me, width)
    rows = jax.ShapeDtypeStruct((span * width, channels), BF16)
    return pl.pallas_call(
        functools.partial(table_kernel, frames, owners),
        out_shape=[jax.ShapeDtypeStruct((group, heads * group), F32), rows, rows],
        in_specs=specs,
        out_specs=[VMEM] * 3,
        scratch_shapes=scratch,
        compiler_params=params(),
        name="tables",
    )(own, latents, cotangent)


def attend_kernel(owners, heads, *refs):
    parts = 2 * owners
    inputs, refs = refs[:parts], refs[parts:]
    pe_ref, table_ref, w_qkv_ref, w_out_ref = refs[:4]
    hidden_ref, cot_ref, dqk_ref, dvo_ref, back_keep, back_send = refs[4:10]
    q_ref, k_ref, v_ref, g_ref = refs[10:]

    core = lax.axis_index("sub")
    rows, channels = hidden_ref.shape
    width = q_ref.shape[1]
    size = width // heads
    group = table_ref.shape[0]
    span = pe_ref.shape[0] // owners
    chunk = rows // owners
    piece = group // owners
    inv_root = 1.0 / math.sqrt(size)

    for step in range(owners):
        at = slice(step * chunk, (step + 1) * chunk)
        first, second = inputs[2 * step][...], inputs[2 * step + 1][...]
        if step == 0:
            lat, cot = first, second
        else:
            lat = jnp.where(core == 0, first, second)
            cot = jnp.where(core == 0, second, first)
        pe = pe_ref[step * span : (step + 1) * span, :]
        lat = lat.astype(F32).reshape(chunk // span, span, channels) + pe[None]
        hidden_ref[at, :] = lat.reshape(chunk, channels).astype(BF16)
        cot_ref[at, :] = cot

    hidden = hidden_ref[...]
    for t, ref in enumerate((q_ref, k_ref, v_ref)):
        ref[...] = dot_nt(hidden, w_qkv_ref[t]).astype(BF16)
    g_ref[...] = dot_nt(cot_ref[...], w_out_ref[...]).astype(BF16)

    lane = lax.broadcasted_iota(jnp.int32, (group, width), 1)
    masks = [(lane >= h * size) & (lane < (h + 1) * size) for h in range(heads)]
    zero = jnp.zeros((group, width), BF16)

    def stack(value):
        return jnp.concatenate([jnp.where(mask, value, zero) for mask in masks], axis=0)

    def flip(value):
        return jnp.concatenate(
            [value[:, h * group : (h + 1) * group].T for h in range(heads)], axis=1
        )

    for start in range(0, chunk, piece):
        spans = [slice(k * chunk + start, k * chunk + start + piece) for k in range(owners)]

        def rows_of(ref, spans=spans):
            return jnp.concatenate([ref[at, :] for at in spans], axis=0)

        def put(ref, value, spans=spans):
            for k, at in enumerate(spans):
                ref[at, :] = value[k * piece : (k + 1) * piece, :]

        query, key, value, grad = rows_of(q_ref), rows_of(k_ref), rows_of(v_ref), rows_of(g_ref)
        keys, values = stack(key), stack(value)
        scores = dot_nt(query, keys) * inv_root + table_ref[...]
        grad_probs = dot_nt(grad, values)
        low, grad_scores = [], []
        for h in range(heads):
            part = slice(h * group, (h + 1) * group)
            own = scores[:, part]
            raw = jnp.exp(own - jnp.max(own, axis=1, keepdims=True))
            probs = raw / jnp.sum(raw, axis=1, keepdims=True)
            up = grad_probs[:, part]
            row_dot = jnp.sum(probs * up, axis=1, keepdims=True)
            low.append(probs.astype(BF16))
            grad_scores.append((probs * (up - row_dot) * inv_root).astype(BF16))
        low = jnp.concatenate(low, axis=1)
        grad_scores = jnp.concatenate(grad_scores, axis=1)
        attn_out = dot_nn(low, values)
        grad_query = dot_nn(grad_scores, keys)
        grad_key = dot_nn(flip(grad_scores), stack(query))
        grad_value = dot_nn(flip(low), stack(grad))
        put(dqk_ref, jnp.concatenate([grad_query, grad_key], axis=1).astype(BF16))
        put(dvo_ref, jnp.concatenate([grad_value, attn_out], axis=1).astype(BF16))

    grad_v = dvo_ref[:, :width]
    back = dot_nn(dqk_ref[...], w_qkv_ref[0:2].reshape(2 * width, channels))
    back = (back + dot_nn(grad_v, w_qkv_ref[2])).astype(BF16).astype(F32)
    lower, upper = back[:, :width], back[:, width:]
    cot = cot_ref[...].astype(F32)

    def store(own, other, base):
        for k in range(owners):
            slot = (owners - k) % owners
            at = slice(k * chunk, (k + 1) * chunk)
            back_keep[slot] = own[at, :] + base[at, :]
            back_send[slot] = other[at, :].astype(BF16)

    @pl.when(core == 0)
    def _():
        store(lower, upper, cot[:, :width])

    @pl.when(core != 0)
    def _():
        store(upper, lower, cot[:, width:])


def attend(inputs, pe, table, w_qkv, w_out, owners, heads):
    chunk, channels = inputs[0].shape
    rows = chunk * owners
    width = w_qkv.shape[1]
    outs = [
        jax.ShapeDtypeStruct((rows, channels), BF16),
        jax.ShapeDtypeStruct((rows, channels), BF16),
        jax.ShapeDtypeStruct((rows, 2 * width), BF16),
        jax.ShapeDtypeStruct((rows, 2 * width), BF16),
        jax.ShapeDtypeStruct((owners, chunk, width), F32),
        jax.ShapeDtypeStruct((owners, chunk, width), BF16),
    ]
    return pl.pallas_call(
        functools.partial(attend_kernel, owners, heads),
        out_shape=outs,
        in_specs=[VMEM] * (len(inputs) + 4),
        out_specs=[VMEM] * len(outs),
        scratch_shapes=[pltpu.VMEM((rows, width), BF16)] * 4,
        compiler_params=params(),
        name="attend",
    )(*inputs, pe, table, w_qkv, w_out)


def weight_kernel(owners, sides, block, count, *refs):
    lefts, grad_ref, outs = refs[:count], refs[count], refs[count + 1 :]
    me, side = lax.axis_index("tm"), lax.axis_index("rows")
    grads = grad_ref[...]
    full = dot_tn(lefts[0][...], grads)
    if count == 2:
        lane = lax.broadcasted_iota(jnp.int32, full.shape, 1)
        full = jnp.where(lane < full.shape[1] // 2, full, dot_tn(lefts[1][...], grads))
    if block % 16:
        outs[0][...] = full
        return
    for z in range(owners):
        slot = lax.rem(z - me + owners, owners)
        for x in range(sides):
            first = (z * sides + x) * block
            piece = full[first : first + block, :]
            turn = lax.rem(x - side + sides, sides)
            for j in range(sides):

                @pl.when(turn == j)
                def _(piece=piece, j=j, slot=slot):
                    outs[j][slot] = piece if j == 0 else piece.astype(BF16)


def weight_terms(lefts, grads, owners, sides):
    channels, columns = lefts[0].shape[1], grads.shape[1]
    block = channels // (owners * sides)
    if block % 16 == 0:
        keep = jax.ShapeDtypeStruct((owners, block, columns), F32)
        outs = [keep] + [jax.ShapeDtypeStruct((owners, block, columns), BF16)] * (sides - 1)
    else:
        outs = [jax.ShapeDtypeStruct((channels, columns), F32)]
    result = pl.pallas_call(
        functools.partial(weight_kernel, owners, sides, block, len(lefts)),
        out_shape=outs,
        in_specs=[VMEM] * (len(lefts) + 1),
        out_specs=[VMEM] * len(outs),
        compiler_params=params(),
        name="weight_terms",
    )(*lefts, grads)
    if block % 16 == 0:
        return result[0], list(result[1:])
    full = result[0].reshape(owners, sides, block, columns)
    full = jnp.roll(full, (-lax.axis_index("tm"), -lax.axis_index("rows")), (0, 1))
    return full[:, 0], [full[:, j].astype(BF16) for j in range(1, sides)]


def combine_kernel(keep_ref, *refs):
    owners = keep_ref.shape[0]
    arrived, outs = refs[: len(refs) - owners], refs[len(refs) - owners :]
    for slot in range(owners):
        total = keep_ref[slot]
        for ref in arrived:
            total = total + ref[slot].astype(F32)
        outs[slot][...] = total.astype(outs[slot].dtype)


def combine(keep, arrived, own_dtype):
    owners = keep.shape[0]
    outs = [jax.ShapeDtypeStruct(keep.shape[1:], own_dtype)]
    outs += [jax.ShapeDtypeStruct(keep.shape[1:], BF16)] * (owners - 1)
    result = pl.pallas_call(
        combine_kernel,
        out_shape=outs,
        in_specs=[VMEM] * (1 + len(arrived)),
        out_specs=[VMEM] * owners,
        compiler_params=params(),
        name="combine",
    )(keep, *arrived)
    return result[0], result[1:]


def finish_kernel(count, *refs):
    ins, (w_qkv_ref, w_out_ref) = refs[:-2], refs[-2:]

    def total(parts):
        value = parts[0][...]
        for ref in parts[1:]:
            value = value + ref[...].astype(F32)
        return value

    width = w_out_ref.shape[1]
    value_out, query_key = total(ins[:count]), total(ins[count:])
    w_qkv_ref[0] = query_key[:, :width]
    w_qkv_ref[1] = query_key[:, width:]
    w_qkv_ref[2] = value_out[:, :width]
    w_out_ref[...] = value_out[:, width:]


def finish(value_out, query_key):
    block, width = value_out[0].shape[0], value_out[0].shape[1] // 2
    count = len(value_out)
    w_qkv, w_out = pl.pallas_call(
        functools.partial(finish_kernel, count),
        out_shape=[
            jax.ShapeDtypeStruct((3, block, width), F32),
            jax.ShapeDtypeStruct((block, width), F32),
        ],
        in_specs=[VMEM] * (2 * count),
        out_specs=[VMEM] * 2,
        compiler_params=params(),
        name="finish",
    )(*value_out, *query_key)
    return jnp.transpose(w_qkv, (1, 0, 2)), w_out


def place_kernel(*refs):
    blocks, out_ref = refs[:-1], refs[-1]
    count = len(blocks)
    frames, positions, channels = out_ref.shape
    width = positions // count
    me = lax.axis_index("tm")
    order = by_position(frames, width, back=True)
    for step, ref in enumerate(blocks):
        start = pl.multiple_of(lax.rem(me - step + count, count) * width, width)
        rows = dot_nn(order, ref[...]).astype(BF16)
        out_ref[:, pl.ds(start, width), :] = rows.reshape(frames, width, channels)


def place(blocks, frames):
    count = len(blocks)
    chunk, channels = blocks[0].shape
    width = chunk // frames
    if width % 16 == 0:
        return pl.pallas_call(
            place_kernel,
            out_shape=jax.ShapeDtypeStruct((frames, count * width, channels), BF16),
            in_specs=[VMEM] * count,
            out_specs=VMEM,
            compiler_params=params(),
            name="place",
        )(*blocks)
    ordered = jnp.roll(jnp.stack(blocks[::-1]), lax.axis_index("tm") + 1, 0)
    ordered = ordered.reshape(count, width, frames, channels)
    return jnp.transpose(ordered, (2, 0, 1, 3)).reshape(frames, count * width, channels)


def per_device(latents, cotangent, w_qkv, w_out, time_bias):
    span, positions, channels = latents.shape
    owners, sides = lax.axis_size("tm"), lax.axis_size("rows")
    frames = span * owners
    heads = H // lax.axis_size("sub")
    group = max(frames, 128)
    me = lax.axis_index("tm")

    sends = send_blocks(latents, cotangent, owners)
    table, own_lat, own_cot = tables(time_bias, latents, cotangent, heads, owners, group)
    owner = lax.rem(me - jnp.arange(owners, dtype=jnp.int32) + owners, owners)
    frame_pos = owner[:, None] * span + jnp.arange(span, dtype=jnp.int32)[None]
    pe = positional(frame_pos.reshape(-1), channels)
    inputs = [own_lat, own_cot]
    for step, block in enumerate(sends):
        mine = shift_send(block, "tm", step + 1)
        inputs += [mine, shift_send(mine, "sub", 1)]
    hidden, cot, grad_qk, grad_vo, back_keep, back_send = attend(
        inputs, pe, table, jnp.transpose(w_qkv, (1, 2, 0)), w_out, owners, heads
    )

    own_back, back_blocks = combine(back_keep, [shift_send(back_send, "sub", 1)], BF16)
    back_blocks = [own_back] + [
        shift_send(block, "tm", step + 1) for step, block in enumerate(back_blocks)
    ]
    sums = []
    for lefts, grads in (((hidden, cot), grad_vo), ((hidden,), grad_qk)):
        if grads is grad_qk:
            grads, _ = lax.optimization_barrier((grads, own_back))
        keep, side_blocks = weight_terms(lefts, grads, owners, sides)
        arrived = [shift_send(b, "rows", j + 1) for j, b in enumerate(side_blocks)]
        if grads is grad_vo:
            arrived, back_blocks = lax.optimization_barrier((arrived, back_blocks))
        own, blocks = combine(keep, arrived, F32)
        sums.append([own] + [shift_send(b, "tm", step + 1) for step, b in enumerate(blocks)])
    grad_w_qkv, grad_w_out_t = finish(*sums)
    return (place(back_blocks, span), grad_w_qkv, grad_w_out_t)


def solution(mesh):
    return jax.shard_map(
        per_device,
        mesh=mesh,
        in_specs=(
            P("tm", ("req", "rows"), None),
            P("tm", ("req", "rows"), None),
            P(None, None, "sub"),
            P("sub", None),
            P(),
        ),
        out_specs=(
            P("tm", ("req", "rows"), "sub"),
            P(("req", "tm", "rows"), None, "sub"),
            P(("req", "tm", "rows"), "sub"),
        ),
        check_vma=False,
    )
```

```python
import functools
import math

import jax
import jax.numpy as jnp
from jax import lax
from jax.experimental import pallas as pl
from jax.experimental.pallas import tpu as pltpu
from jax.sharding import PartitionSpec as P

H = 8
VMEM = pl.BlockSpec(memory_space=pltpu.VMEM)
BF16 = jnp.bfloat16
F32 = jnp.float32


def params(limit=48 << 20):
    return pltpu.CompilerParams(vmem_limit_bytes=limit)


def shift_send(array, axis, step):
    size = lax.axis_size(axis)
    return lax.ppermute(array, axis, [(i, (i + step) % size) for i in range(size)])


def dot_nn(a, b):
    return lax.dot_general(a, b, (((1,), (0,)), ((), ())), preferred_element_type=F32)


def dot_nt(a, b):
    return lax.dot_general(a, b, (((1,), (1,)), ((), ())), preferred_element_type=F32)


def dot_tn(a, b):
    return lax.dot_general(a, b, (((0,), (0,)), ((), ())), preferred_element_type=F32)


def positional(frame_pos, channels):
    half = channels // 2
    frequency = jnp.exp(-math.log(10000.0) * jnp.arange(half, dtype=F32) * 2.0 / channels)
    angles = frame_pos.astype(F32)[:, None] * frequency[None, :]
    return jnp.concatenate((jnp.sin(angles), jnp.cos(angles)), axis=1)


def by_position(frames, width, back=False):
    rows = frames * width
    inner = width if back else frames
    outer = rows // inner
    row = lax.broadcasted_iota(jnp.int32, (rows, 1), 0)
    col = lax.broadcasted_iota(jnp.int32, (rows, rows), 1)
    source = lax.rem(row, inner) * outer + lax.div(row, inner)
    return jnp.where(col == source, 1.0, 0.0).astype(BF16)


def table_kernel(frames, owners, bias_ref, table_ref):
    heads, lanes = bias_ref.shape
    group = table_ref.shape[0]
    span = frames // owners
    me = lax.axis_index("tm")

    def place_of(index):
        return lax.rem(lax.div(index, span), group // frames)

    def frame_of(index):
        owner = lax.rem(me - lax.div(index, group // owners) + owners, owners)
        return owner * span + lax.rem(index, span)

    row = lax.broadcasted_iota(jnp.int32, (group, 1), 0)
    col = lax.broadcasted_iota(jnp.int32, (1, group), 1)
    same = place_of(row) == place_of(col)
    left = jnp.where(frame_of(row) == col, 1.0, 0.0)
    right = jnp.where(row == frame_of(col), 1.0, 0.0)

    def exact(a, b):
        return lax.dot_general(
            a, b, (((1,), (0,)), ((), ())), precision=lax.Precision.HIGHEST,
            preferred_element_type=F32,
        )

    for h in range(heads):
        spread = jnp.broadcast_to(bias_ref[h : h + 1, :], (group, lanes))
        skewed = pltpu.roll(spread, (1 - frames) % lanes, 1, stride=1, stride_axis=0)
        turned_bias = exact(left, exact(skewed[:, :group], right))
        table_ref[:, h * group : (h + 1) * group] = jnp.where(same, turned_bias, -1e30)


def send_blocks(latents, cotangent, count, parts):
    frames, positions, _ = latents.shape
    width = positions // count
    me = lax.axis_index("tm")
    sent = jnp.where(lax.axis_index("sub") == 0, latents, cotangent)
    blocks = [cut(sent, lax.rem(me + step, count), width) for step in range(1, count)]
    first, sends = 0, []
    for part in parts:
        sends.append([b[first : first + frames * part] for b in blocks])
        first += frames * part
    return sends


def cut(array, owner, width):
    block = lax.dynamic_slice_in_dim(array, owner * width, width, 1)
    return jnp.swapaxes(block, 0, 1).reshape(-1, array.shape[2])


def bias_of_rows(time_bias, heads, frames, owners, group):
    own = lax.dynamic_slice_in_dim(time_bias, lax.axis_index("sub") * heads, heads, 0)
    lanes = -(-max(2 * frames - 1, group) // 128) * 128
    own = jnp.pad(own, ((0, 0), (0, lanes - own.shape[1])))
    return pl.pallas_call(
        functools.partial(table_kernel, frames, owners),
        out_shape=jax.ShapeDtypeStruct((group, heads * group), F32),
        in_specs=[VMEM],
        out_specs=VMEM,
        compiler_params=params(),
        name="bias_of_rows",
    )(own)


def attend_kernel(owners, heads, *refs):
    parts = 2 * owners
    inputs, refs = refs[:parts], refs[parts:]
    pe_ref, table_ref, w_qkv_ref, w_out_ref = refs[:4]
    hidden_ref, cot_ref, dqk_ref, dvo_ref, back_keep, back_send = refs[4:10]
    q_ref, k_ref, v_ref, g_ref = refs[10:]

    core = lax.axis_index("sub")
    rows, channels = hidden_ref.shape
    width = q_ref.shape[1]
    size = width // heads
    group = table_ref.shape[0]
    span = pe_ref.shape[0] // owners
    chunk = rows // owners
    piece = group // owners
    inv_root = 1.0 / math.sqrt(size)

    for step in range(owners):
        at = slice(step * chunk, (step + 1) * chunk)
        first, second = inputs[2 * step][...], inputs[2 * step + 1][...]
        if step == 0:
            lat, cot = first, second
        else:
            lat = jnp.where(core == 0, first, second)
            cot = jnp.where(core == 0, second, first)
        pe = pe_ref[step * span : (step + 1) * span, :]
        lat = lat.astype(F32).reshape(chunk // span, span, channels) + pe[None]
        hidden_ref[at, :] = lat.reshape(chunk, channels).astype(BF16)
        cot_ref[at, :] = cot

    hidden = hidden_ref[...]
    qkv = dot_nt(hidden, w_qkv_ref[...].reshape(3 * width, channels)).astype(BF16)
    for t, ref in enumerate((q_ref, k_ref, v_ref)):
        ref[...] = qkv[:, t * width : (t + 1) * width]
    g_ref[...] = dot_nt(cot_ref[...], w_out_ref[...]).astype(BF16)

    lane = lax.broadcasted_iota(jnp.int32, (group, width), 1)
    masks = [(lane >= h * size) & (lane < (h + 1) * size) for h in range(heads)]
    zero = jnp.zeros((group, width), BF16)

    def stack(value):
        return jnp.concatenate([jnp.where(mask, value, zero) for mask in masks], axis=0)

    def flip(value):
        return jnp.concatenate(
            [value[:, h * group : (h + 1) * group].T for h in range(heads)], axis=1
        )

    for start in range(0, chunk, piece):
        spans = [slice(k * chunk + start, k * chunk + start + piece) for k in range(owners)]

        def rows_of(ref, spans=spans):
            return jnp.concatenate([ref[at, :] for at in spans], axis=0)

        def put(ref, value, spans=spans):
            for k, at in enumerate(spans):
                ref[at, :] = value[k * piece : (k + 1) * piece, :]

        query, key, value, grad = rows_of(q_ref), rows_of(k_ref), rows_of(v_ref), rows_of(g_ref)
        queries, grads = stack(query), stack(grad)
        scores = dot_nt(key, queries) * inv_root + table_ref[...]
        grad_probs = dot_nt(value, grads)
        raw = jnp.exp(scores - jnp.max(scores, axis=0, keepdims=True))
        probs = raw / jnp.sum(raw, axis=0, keepdims=True)
        row_dot = jnp.sum(probs * grad_probs, axis=0, keepdims=True)
        low = probs.astype(BF16)
        grad_scores = (probs * (grad_probs - row_dot) * inv_root).astype(BF16)
        grad_key = dot_nn(grad_scores, queries)
        grad_value = dot_nn(low, grads)
        grad_query = dot_nn(flip(grad_scores), stack(key))
        attn_out = dot_nn(flip(low), stack(value))
        put(dqk_ref, jnp.concatenate([grad_query, grad_key], axis=1).astype(BF16))
        put(dvo_ref, jnp.concatenate([grad_value, attn_out], axis=1).astype(BF16))

    grad_v = dvo_ref[:, :width]
    back = dot_nn(dqk_ref[...], w_qkv_ref[0:2].reshape(2 * width, channels))
    back = (back + dot_nn(grad_v, w_qkv_ref[2])).astype(BF16).astype(F32)
    lower, upper = back[:, :width], back[:, width:]
    cot = cot_ref[...].astype(F32)

    def store(own, other, base):
        for k in range(owners):
            slot = (owners - k) % owners
            at = slice(k * chunk, (k + 1) * chunk)
            back_keep[slot] = own[at, :] + base[at, :]
            back_send[slot] = other[at, :].astype(BF16)

    @pl.when(core == 0)
    def _():
        store(lower, upper, cot[:, :width])

    @pl.when(core != 0)
    def _():
        store(upper, lower, cot[:, width:])


def attend(inputs, pe, table, w_qkv, w_out, owners, heads):
    chunk, channels = inputs[0].shape
    rows = chunk * owners
    width = w_qkv.shape[1]
    outs = [
        jax.ShapeDtypeStruct((rows, channels), BF16),
        jax.ShapeDtypeStruct((rows, channels), BF16),
        jax.ShapeDtypeStruct((rows, 2 * width), BF16),
        jax.ShapeDtypeStruct((rows, 2 * width), BF16),
        jax.ShapeDtypeStruct((owners, chunk, width), F32),
        jax.ShapeDtypeStruct((owners, chunk, width), BF16),
    ]
    return pl.pallas_call(
        functools.partial(attend_kernel, owners, heads),
        out_shape=outs,
        in_specs=[VMEM] * (len(inputs) + 4),
        out_specs=[VMEM] * len(outs),
        scratch_shapes=[pltpu.VMEM((rows, width), BF16)] * 4,
        compiler_params=params(),
        name="attend",
    )(*inputs, pe, table, w_qkv, w_out)


def weight_kernel(owners, sides, block, parts, count, *refs):
    grads, lefts, outs = refs[:parts], refs[parts : parts + count], refs[parts + count :]
    me, side = lax.axis_index("tm"), lax.axis_index("rows")
    values = [ref[...] for ref in grads]

    def product(lefts):
        total = dot_tn(lefts[0][...], values[0])
        for left, value in zip(lefts[1:], values[1:]):
            total = total + dot_tn(left[...], value)
        return total

    full = product(lefts[:parts])
    if count > parts:
        lane = lax.broadcasted_iota(jnp.int32, full.shape, 1)
        full = jnp.where(lane < full.shape[1] // 2, full, product(lefts[parts:]))
    if block % 16:
        outs[0][...] = full
        return
    for z in range(owners):
        slot = lax.rem(z - me + owners, owners)
        for x in range(sides):
            first = (z * sides + x) * block
            piece = full[first : first + block, :]
            turn = lax.rem(x - side + sides, sides)
            for j in range(sides):

                @pl.when(turn == j)
                def _(piece=piece, j=j, slot=slot):
                    outs[j][slot] = piece if j == 0 else piece.astype(BF16)


def weight_terms(grads, lefts, owners, sides):
    channels, columns = lefts[0].shape[1], grads[0].shape[1]
    block = channels // (owners * sides)
    if block % 16 == 0:
        keep = jax.ShapeDtypeStruct((owners, block, columns), F32)
        outs = [keep] + [jax.ShapeDtypeStruct((owners, block, columns), BF16)] * (sides - 1)
    else:
        outs = [jax.ShapeDtypeStruct((channels, columns), F32)]
    result = pl.pallas_call(
        functools.partial(weight_kernel, owners, sides, block, len(grads), len(lefts)),
        out_shape=outs,
        in_specs=[VMEM] * (len(grads) + len(lefts)),
        out_specs=[VMEM] * len(outs),
        compiler_params=params(),
        name="weight_terms",
    )(*grads, *lefts)
    if block % 16 == 0:
        return result[0], list(result[1:])
    full = result[0].reshape(owners, sides, block, columns)
    full = jnp.roll(full, (-lax.axis_index("tm"), -lax.axis_index("rows")), (0, 1))
    return full[:, 0], [full[:, j].astype(BF16) for j in range(1, sides)]


def combine_kernel(keep_ref, *refs):
    owners = keep_ref.shape[0]
    arrived, outs = refs[: len(refs) - owners], refs[len(refs) - owners :]
    for slot in range(owners):
        total = keep_ref[slot]
        for ref in arrived:
            total = total + ref[slot].astype(F32)
        outs[slot][...] = total.astype(outs[slot].dtype)


def combine(keep, arrived):
    owners = keep.shape[0]
    outs = [jax.ShapeDtypeStruct(keep.shape[1:], F32)]
    outs += [jax.ShapeDtypeStruct(keep.shape[1:], BF16)] * (owners - 1)
    result = pl.pallas_call(
        combine_kernel,
        out_shape=outs,
        in_specs=[VMEM] * (1 + len(arrived)),
        out_specs=[VMEM] * owners,
        compiler_params=params(),
        name="combine",
    )(keep, *arrived)
    return result[0], result[1:]


def join_kernel(parts, *refs):
    keeps, arrived, outs = refs[:parts], refs[parts : 2 * parts], refs[2 * parts :]
    for slot, out in enumerate(outs):
        sums = [keep[slot] + ref[slot].astype(F32) for keep, ref in zip(keeps, arrived)]
        total = jnp.concatenate(sums, axis=0)
        half = total.shape[0] // 2
        out[...] = jnp.concatenate([total[:half], total[half:]], axis=1).astype(BF16)


def join(keeps, arrived):
    owners, _, width = keeps[0].shape
    rows = sum(keep.shape[1] for keep in keeps)
    return pl.pallas_call(
        functools.partial(join_kernel, len(keeps)),
        out_shape=[jax.ShapeDtypeStruct((rows // 2, 2 * width), BF16)] * owners,
        in_specs=[VMEM] * (2 * len(keeps)),
        out_specs=[VMEM] * owners,
        compiler_params=params(),
        name="join",
    )(*keeps, *arrived)


def finish_kernel(count, *refs):
    ins, (w_qkv_ref, w_out_ref) = refs[:-2], refs[-2:]

    def total(parts):
        value = parts[0][...]
        for ref in parts[1:]:
            value = value + ref[...].astype(F32)
        return value

    width = w_out_ref.shape[1]
    value_out, query_key = total(ins[:count]), total(ins[count:])
    w_qkv_ref[0] = query_key[:, :width]
    w_qkv_ref[1] = query_key[:, width:]
    w_qkv_ref[2] = value_out[:, :width]
    w_out_ref[...] = value_out[:, width:]


def finish(value_out, query_key):
    block, width = value_out[0].shape[0], value_out[0].shape[1] // 2
    count = len(value_out)
    w_qkv, w_out = pl.pallas_call(
        functools.partial(finish_kernel, count),
        out_shape=[
            jax.ShapeDtypeStruct((3, block, width), F32),
            jax.ShapeDtypeStruct((block, width), F32),
        ],
        in_specs=[VMEM] * (2 * count),
        out_specs=[VMEM] * 2,
        compiler_params=params(),
        name="finish",
    )(*value_out, *query_key)
    return jnp.transpose(w_qkv, (1, 0, 2)), w_out


def place_kernel(*refs):
    blocks, out_ref = refs[:-1], refs[-1]
    count = len(blocks)
    frames, positions, channels = out_ref.shape
    width = positions // count
    me = lax.axis_index("tm")
    order = by_position(frames, width, back=True)
    for step, ref in enumerate(blocks):
        start = pl.multiple_of(lax.rem(me - step + count, count) * width, width)
        rows = dot_nn(order, unfold(ref[...])).astype(BF16)
        out_ref[:, pl.ds(start, width), :] = rows.reshape(frames, width, channels)


def unfold(block):
    channels = block.shape[1] // 2
    return jnp.concatenate([block[:, :channels], block[:, channels:]], axis=0)


def place(blocks, frames):
    count = len(blocks)
    chunk, channels = 2 * blocks[0].shape[0], blocks[0].shape[1] // 2
    width = chunk // frames
    if width % 16 == 0:
        return pl.pallas_call(
            place_kernel,
            out_shape=jax.ShapeDtypeStruct((frames, count * width, channels), BF16),
            in_specs=[VMEM] * count,
            out_specs=VMEM,
            compiler_params=params(),
            name="place",
        )(*blocks)
    ordered = jnp.stack([unfold(b) for b in blocks[::-1]])
    ordered = jnp.roll(ordered, lax.axis_index("tm") + 1, 0)
    ordered = ordered.reshape(count, width, frames, channels)
    return jnp.transpose(ordered, (2, 0, 1, 3)).reshape(frames, count * width, channels)


def per_device(latents, cotangent, w_qkv, w_out, time_bias):
    span, positions, channels = latents.shape
    owners, sides = lax.axis_size("tm"), lax.axis_size("rows")
    frames = span * owners
    heads = H // lax.axis_size("sub")
    group = max(frames, 128)
    me = lax.axis_index("tm")

    parts = [positions // owners]

    sends = send_blocks(latents, cotangent, owners, parts)
    table = bias_of_rows(time_bias, heads, frames, owners, group)
    own_lat, own_cot = ([cut(a, me, positions // owners)] for a in (latents, cotangent))
    owner = lax.rem(me - jnp.arange(owners, dtype=jnp.int32) + owners, owners)
    frame_pos = owner[:, None] * span + jnp.arange(span, dtype=jnp.int32)[None]
    pe = positional(frame_pos.reshape(-1), channels)
    w_rows = jnp.transpose(w_qkv, (1, 2, 0))
    results = []
    for at, blocks in enumerate(sends):
        inputs = [own_lat[at], own_cot[at]]
        for step, block in enumerate(blocks):
            mine = shift_send(block, "tm", step + 1)
            inputs += [mine, shift_send(mine, "sub", 1)]
        results.append(attend(inputs, pe, table, w_rows, w_out, owners, heads))
    hidden, cot, grad_qk, grad_vo, back_keep, back_send = (list(r) for r in zip(*results))

    back_send = lax.optimization_barrier(back_send)
    back_blocks = join(back_keep, [shift_send(b, "sub", 1) for b in back_send])
    own_back = back_blocks[0]
    back_blocks = [own_back] + [
        shift_send(block, "tm", step + 1) for step, block in enumerate(back_blocks[1:])
    ]
    sums = []
    for lefts, grads in ((hidden + cot, grad_vo), (hidden, grad_qk)):
        if grads is grad_qk:
            grads, own_back = lax.optimization_barrier((grads, own_back))
        keep, side_blocks = weight_terms(grads, lefts, owners, sides)
        arrived = [shift_send(b, "rows", j + 1) for j, b in enumerate(side_blocks)]
        if grads is grad_vo:
            arrived, back_blocks = lax.optimization_barrier((arrived, back_blocks))
        own, blocks = combine(keep, arrived)
        sums.append([own] + [shift_send(b, "tm", step + 1) for step, b in enumerate(blocks)])
    grad_w_qkv, grad_w_out_t = finish(*sums)
    return (place(back_blocks, span), grad_w_qkv, grad_w_out_t)


def solution(mesh):
    return jax.shard_map(
        per_device,
        mesh=mesh,
        in_specs=(
            P("tm", ("req", "rows"), None),
            P("tm", ("req", "rows"), None),
            P(None, None, "sub"),
            P("sub", None),
            P(),
        ),
        out_specs=(
            P("tm", ("req", "rows"), "sub"),
            P(("req", "tm", "rows"), None, "sub"),
            P(("req", "tm", "rows"), "sub"),
        ),
        check_vma=False,
    )
```

```python
import functools
import math

import jax
import jax.numpy as jnp
from jax import lax
from jax.experimental import pallas as pl
from jax.experimental.pallas import tpu as pltpu
from jax.sharding import PartitionSpec as P

H = 8
VMEM = pl.BlockSpec(memory_space=pltpu.VMEM)
BF16 = jnp.bfloat16
F32 = jnp.float32


def params(limit=48 << 20):
    return pltpu.CompilerParams(vmem_limit_bytes=limit)


def shift_send(array, axis, step):
    size = lax.axis_size(axis)
    return lax.ppermute(array, axis, [(i, (i + step) % size) for i in range(size)])


def dot_nn(a, b):
    return lax.dot_general(a, b, (((1,), (0,)), ((), ())), preferred_element_type=F32)


def dot_nt(a, b):
    return lax.dot_general(a, b, (((1,), (1,)), ((), ())), preferred_element_type=F32)


def dot_tn(a, b):
    return lax.dot_general(a, b, (((0,), (0,)), ((), ())), preferred_element_type=F32)


def positional(frame_pos, channels):
    half = channels // 2
    frequency = jnp.exp(-math.log(10000.0) * jnp.arange(half, dtype=F32) * 2.0 / channels)
    angles = frame_pos.astype(F32)[:, None] * frequency[None, :]
    return jnp.concatenate((jnp.sin(angles), jnp.cos(angles)), axis=1)


def by_position(frames, width, back=False):
    rows = frames * width
    inner = width if back else frames
    outer = rows // inner
    row = lax.broadcasted_iota(jnp.int32, (rows, 1), 0)
    col = lax.broadcasted_iota(jnp.int32, (rows, rows), 1)
    source = lax.rem(row, inner) * outer + lax.div(row, inner)
    return jnp.where(col == source, 1.0, 0.0).astype(BF16)


def table_kernel(frames, owners, bias_ref, table_ref):
    heads, lanes = bias_ref.shape
    group = table_ref.shape[0]
    span = frames // owners
    me = lax.axis_index("tm")

    def place_of(index):
        return lax.rem(lax.div(index, span), group // frames)

    def frame_of(index):
        owner = lax.rem(me - lax.div(index, group // owners) + owners, owners)
        return owner * span + lax.rem(index, span)

    row = lax.broadcasted_iota(jnp.int32, (group, 1), 0)
    col = lax.broadcasted_iota(jnp.int32, (1, group), 1)
    same = place_of(row) == place_of(col)
    left = jnp.where(frame_of(row) == col, 1.0, 0.0)
    right = jnp.where(row == frame_of(col), 1.0, 0.0)

    def exact(a, b):
        return lax.dot_general(
            a, b, (((1,), (0,)), ((), ())), precision=lax.Precision.HIGHEST,
            preferred_element_type=F32,
        )

    for h in range(heads):
        spread = jnp.broadcast_to(bias_ref[h : h + 1, :], (group, lanes))
        skewed = pltpu.roll(spread, (1 - frames) % lanes, 1, stride=1, stride_axis=0)
        turned_bias = exact(left, exact(skewed[:, :group], right))
        table_ref[:, h * group : (h + 1) * group] = jnp.where(same, turned_bias, -1e30)


def send_blocks(latents, cotangent, count):
    width = latents.shape[1] // count
    me = lax.axis_index("tm")
    sent = jnp.where(lax.axis_index("sub") == 0, latents, cotangent)
    return [cut(sent, lax.rem(me + step, count), width) for step in range(1, count)]


def cut(array, owner, width):
    block = lax.dynamic_slice_in_dim(array, owner * width, width, 1)
    return jnp.swapaxes(block, 0, 1).reshape(-1, array.shape[2])


def bias_of_rows(time_bias, heads, frames, owners, group):
    own = lax.dynamic_slice_in_dim(time_bias, lax.axis_index("sub") * heads, heads, 0)
    lanes = -(-max(2 * frames - 1, group) // 128) * 128
    own = jnp.pad(own, ((0, 0), (0, lanes - own.shape[1])))
    return pl.pallas_call(
        functools.partial(table_kernel, frames, owners),
        out_shape=jax.ShapeDtypeStruct((group, heads * group), F32),
        in_specs=[VMEM],
        out_specs=VMEM,
        compiler_params=params(),
        name="bias_of_rows",
    )(own)


def attend_kernel(owners, heads, *refs):
    parts = 2 * owners
    inputs, refs = refs[:parts], refs[parts:]
    pe_ref, table_ref, w_qkv_ref, w_out_ref, w_own_ref, w_other_ref = refs[:6]
    hidden_ref, cot_ref, dqk_ref, dvo_ref, back_keep, back_send = refs[6:12]
    q_ref, k_ref, v_ref, g_ref = refs[12:]

    core = lax.axis_index("sub")
    rows, channels = hidden_ref.shape
    width = q_ref.shape[1]
    size = width // heads
    group = table_ref.shape[0]
    span = pe_ref.shape[0] // owners
    chunk = rows // owners
    piece = group // owners
    inv_root = 1.0 / math.sqrt(size)

    for step in range(owners):
        at = slice(step * chunk, (step + 1) * chunk)
        first, second = inputs[2 * step][...], inputs[2 * step + 1][...]
        if step == 0:
            lat, cot = first, second
        else:
            lat = jnp.where(core == 0, first, second)
            cot = jnp.where(core == 0, second, first)
        pe = pe_ref[step * span : (step + 1) * span, :]
        lat = lat.astype(F32).reshape(chunk // span, span, channels) + pe[None]
        hidden_ref[at, :] = lat.reshape(chunk, channels).astype(BF16)
        cot_ref[at, :] = cot

    hidden = hidden_ref[...]
    qkv = dot_nt(hidden, w_qkv_ref[...].reshape(3 * width, channels)).astype(BF16)
    for t, ref in enumerate((q_ref, k_ref, v_ref)):
        ref[...] = qkv[:, t * width : (t + 1) * width]
    g_ref[...] = dot_nt(cot_ref[...], w_out_ref[...]).astype(BF16)

    lane = lax.broadcasted_iota(jnp.int32, (group, width), 1)
    masks = [(lane >= h * size) & (lane < (h + 1) * size) for h in range(heads)]
    zero = jnp.zeros((group, width), BF16)

    def stack(value):
        return jnp.concatenate([jnp.where(mask, value, zero) for mask in masks], axis=0)

    def flip(value):
        return jnp.concatenate(
            [value[:, h * group : (h + 1) * group].T for h in range(heads)], axis=1
        )

    def rows_of(ref, start):
        return jnp.concatenate(
            [ref[k * chunk + start : k * chunk + start + piece, :] for k in range(owners)], axis=0
        )

    def put(ref, start, *halves):
        value = jnp.concatenate(halves, axis=1).astype(BF16)
        for k in range(owners):
            at = k * chunk + start
            ref[at : at + piece, :] = value[k * piece : (k + 1) * piece, :]

    starts = list(range(0, chunk, piece))
    wide = 2
    for some in [starts[i : i + wide] for i in range(0, len(starts), wide)]:
        rows = [[rows_of(ref, at) for ref in (q_ref, k_ref, v_ref, g_ref)] for at in some]
        queries, grads = [stack(r[0]) for r in rows], [stack(r[3]) for r in rows]
        scores = [dot_nt(r[1], q) * inv_root + table_ref[...] for r, q in zip(rows, queries)]
        grad_probs = [dot_nt(r[2], g) for r, g in zip(rows, grads)]
        raw = [jnp.exp(x - jnp.max(x, axis=0, keepdims=True)) for x in scores]
        probs = [x / jnp.sum(x, axis=0, keepdims=True) for x in raw]
        low = [p.astype(BF16) for p in probs]
        grad_value = [dot_nn(p, g) for p, g in zip(low, grads)]
        row_dot = [jnp.sum(p * u, axis=0, keepdims=True) for p, u in zip(probs, grad_probs)]
        grad_scores = [
            (p * (u - d) * inv_root).astype(BF16) for p, u, d in zip(probs, grad_probs, row_dot)
        ]
        attn_out = [dot_nn(flip(p), stack(r[2])) for p, r in zip(low, rows)]
        grad_key = [dot_nn(d, q) for d, q in zip(grad_scores, queries)]
        grad_query = [dot_nn(flip(d), stack(r[1])) for d, r in zip(grad_scores, rows)]
        for n, at in enumerate(some):
            put(dqk_ref, at, grad_query[n], grad_key[n])
            put(dvo_ref, at, grad_value[n], attn_out[n])

    grads = jnp.concatenate([dqk_ref[...], dvo_ref[:, :width]], axis=1)
    for w_ref, back_ref in ((w_own_ref, back_keep), (w_other_ref, back_send)):
        back = dot_nn(grads, w_ref[...]).astype(BF16)
        for k in range(owners):
            back_ref[(owners - k) % owners] = back[k * chunk : (k + 1) * chunk, :]


def attend(inputs, pe, table, w_qkv, w_out, w_back, owners, heads):
    chunk, channels = inputs[0].shape
    rows = chunk * owners
    width = w_qkv.shape[1]
    outs = [
        jax.ShapeDtypeStruct((rows, channels), BF16),
        jax.ShapeDtypeStruct((rows, channels), BF16),
        jax.ShapeDtypeStruct((rows, 2 * width), BF16),
        jax.ShapeDtypeStruct((rows, 2 * width), BF16),
        jax.ShapeDtypeStruct((owners, chunk, width), BF16),
        jax.ShapeDtypeStruct((owners, chunk, width), BF16),
    ]
    return pl.pallas_call(
        functools.partial(attend_kernel, owners, heads),
        out_shape=outs,
        in_specs=[VMEM] * (len(inputs) + 6),
        out_specs=[VMEM] * len(outs),
        scratch_shapes=[pltpu.VMEM((rows, width), BF16)] * 4,
        compiler_params=params(),
        name="attend",
    )(*inputs, pe, table, w_qkv, w_out, *w_back)


def weight_kernel(owners, sides, block, parts, count, *refs):
    grads, lefts, outs = refs[:parts], refs[parts : parts + count], refs[parts + count :]
    me, side = lax.axis_index("tm"), lax.axis_index("rows")
    values = [ref[...] for ref in grads]

    def product(lefts, columns):
        total = dot_tn(lefts[0][...], values[0][:, columns])
        for left, value in zip(lefts[1:], values[1:]):
            total = total + dot_tn(left[...], value[:, columns])
        return total

    columns = values[0].shape[1]
    if count > parts:
        low, high = columns // 2 // 128 * 128, -(-(columns // 2) // 128) * 128
        lower = product(lefts[:parts], slice(0, high))
        upper = product(lefts[parts:], slice(low, columns))
        pieces = [lower[:, :low]]
        if high > low:
            lane = lax.broadcasted_iota(jnp.int32, (lower.shape[0], high - low), 1) + low
            shared = jnp.where(lane < columns // 2, lower[:, low:], upper[:, : high - low])
            pieces.append(shared)
        full = jnp.concatenate(pieces + [upper[:, high - low :]], axis=1)
    else:
        full = product(lefts, slice(0, columns))
    if block % 16:
        outs[0][...] = full
        return
    for z in range(owners):
        slot = lax.rem(z - me + owners, owners)
        rows = [full[(z * sides + x) * block :][:block] for x in range(sides)]
        for j in range(sides):
            turned = rows[j]
            for shift in range(1, sides):
                turned = jnp.where(side == shift, rows[(j + shift) % sides], turned)
            outs[j][slot] = turned if j == 0 else turned.astype(BF16)


def weight_terms(grads, lefts, owners, sides):
    channels, columns = lefts[0].shape[1], grads[0].shape[1]
    block = channels // (owners * sides)
    if block % 16 == 0:
        keep = jax.ShapeDtypeStruct((owners, block, columns), F32)
        outs = [keep] + [jax.ShapeDtypeStruct((owners, block, columns), BF16)] * (sides - 1)
    else:
        outs = [jax.ShapeDtypeStruct((channels, columns), F32)]
    result = pl.pallas_call(
        functools.partial(weight_kernel, owners, sides, block, len(grads), len(lefts)),
        out_shape=outs,
        in_specs=[VMEM] * (len(grads) + len(lefts)),
        out_specs=[VMEM] * len(outs),
        compiler_params=params(),
        name="weight_terms",
    )(*grads, *lefts)
    if block % 16 == 0:
        return result[0], list(result[1:])
    full = result[0].reshape(owners, sides, block, columns)
    full = jnp.roll(full, (-lax.axis_index("tm"), -lax.axis_index("rows")), (0, 1))
    return full[:, 0], [full[:, j].astype(BF16) for j in range(1, sides)]


def combine_kernel(keep_ref, *refs):
    owners = keep_ref.shape[0]
    arrived, outs = refs[: len(refs) - owners], refs[len(refs) - owners :]
    for slot in range(owners):
        total = keep_ref[slot]
        for ref in arrived:
            total = total + ref[slot].astype(F32)
        outs[slot][...] = total.astype(outs[slot].dtype)


def combine(keep, arrived):
    owners = keep.shape[0]
    outs = [jax.ShapeDtypeStruct(keep.shape[1:], F32)]
    outs += [jax.ShapeDtypeStruct(keep.shape[1:], BF16)] * (owners - 1)
    result = pl.pallas_call(
        combine_kernel,
        out_shape=outs,
        in_specs=[VMEM] * (1 + len(arrived)),
        out_specs=[VMEM] * owners,
        compiler_params=params(),
        name="combine",
    )(keep, *arrived)
    return result[0], result[1:]


def join_kernel(keep_ref, arrived_ref, *outs):
    for slot, out in enumerate(outs):
        total = keep_ref[slot].astype(F32) + arrived_ref[slot].astype(F32)
        half = total.shape[0] // 2
        out[...] = jnp.concatenate([total[:half], total[half:]], axis=1).astype(BF16)


def join(keep, arrived):
    owners, rows, width = keep.shape
    return pl.pallas_call(
        join_kernel,
        out_shape=[jax.ShapeDtypeStruct((rows // 2, 2 * width), BF16)] * owners,
        in_specs=[VMEM] * 2,
        out_specs=[VMEM] * owners,
        compiler_params=params(),
        name="join",
    )(keep, arrived)


def finish_kernel(count, *refs):
    ins, (w_qkv_ref, w_out_ref) = refs[:-2], refs[-2:]

    def total(parts):
        value = parts[0][...]
        for ref in parts[1:]:
            value = value + ref[...].astype(F32)
        return value

    width = w_out_ref.shape[1]
    value_out, query_key = total(ins[:count]), total(ins[count:])
    w_qkv_ref[0] = query_key[:, :width]
    w_qkv_ref[1] = query_key[:, width:]
    w_qkv_ref[2] = value_out[:, :width]
    w_out_ref[...] = value_out[:, width:]


def finish(value_out, query_key):
    block, width = value_out[0].shape[0], value_out[0].shape[1] // 2
    count = len(value_out)
    w_qkv, w_out = pl.pallas_call(
        functools.partial(finish_kernel, count),
        out_shape=[
            jax.ShapeDtypeStruct((3, block, width), F32),
            jax.ShapeDtypeStruct((block, width), F32),
        ],
        in_specs=[VMEM] * (2 * count),
        out_specs=[VMEM] * 2,
        compiler_params=params(),
        name="finish",
    )(*value_out, *query_key)
    return jnp.transpose(w_qkv, (1, 0, 2)), w_out


def place_kernel(*refs):
    blocks, cot_ref, out_ref = refs[:-2], refs[-2], refs[-1]
    count = len(blocks)
    frames, positions, channels = out_ref.shape
    width = positions // count
    me = lax.axis_index("tm")
    order = by_position(frames, width, back=True)
    for step, ref in enumerate(blocks):
        start = pl.multiple_of(lax.rem(me - step + count, count) * width, width)
        rows = dot_nn(order, unfold(ref[...])).reshape(frames, width, channels)
        at = pl.ds(start, width)
        out_ref[:, at, :] = (cot_ref[:, at, :].astype(F32) + rows).astype(BF16)


def unfold(block):
    channels = block.shape[1] // 2
    return jnp.concatenate([block[:, :channels], block[:, channels:]], axis=0)


def place(blocks, cot):
    frames = cot.shape[0]
    count = len(blocks)
    chunk, channels = 2 * blocks[0].shape[0], blocks[0].shape[1] // 2
    width = chunk // frames
    if width % 16 == 0:
        return pl.pallas_call(
            place_kernel,
            out_shape=jax.ShapeDtypeStruct((frames, count * width, channels), BF16),
            in_specs=[VMEM] * (count + 1),
            out_specs=VMEM,
            compiler_params=params(),
            name="place",
        )(*blocks, cot)
    ordered = jnp.stack([unfold(b) for b in blocks[::-1]])
    ordered = jnp.roll(ordered, lax.axis_index("tm") + 1, 0)
    ordered = ordered.reshape(count, width, frames, channels)
    moved = jnp.transpose(ordered, (2, 0, 1, 3)).reshape(frames, count * width, channels)
    return (cot.astype(F32) + moved.astype(F32)).astype(BF16)


def per_device(latents, cotangent, w_qkv, w_out, time_bias):
    span, positions, channels = latents.shape
    owners, sides = lax.axis_size("tm"), lax.axis_size("rows")
    frames = span * owners
    heads = H // lax.axis_size("sub")
    group = max(frames, 128)
    me = lax.axis_index("tm")

    core = lax.axis_index("sub")
    width = w_qkv.shape[2]

    sends = send_blocks(latents, cotangent, owners)
    table = bias_of_rows(time_bias, heads, frames, owners, group)
    inputs = [cut(a, me, positions // owners) for a in (latents, cotangent)]
    owner = lax.rem(me - jnp.arange(owners, dtype=jnp.int32) + owners, owners)
    frame_pos = owner[:, None] * span + jnp.arange(span, dtype=jnp.int32)[None]
    pe = positional(frame_pos.reshape(-1), channels)
    w_rows = jnp.transpose(w_qkv, (1, 2, 0))
    w_flat = w_rows.reshape(3 * width, channels)
    w_back = [
        lax.dynamic_slice_in_dim(w_flat, which * width, width, 1) for which in (core, 1 - core)
    ]
    for step, block in enumerate(sends):
        mine = shift_send(block, "tm", step + 1)
        if step == 0:
            mine, w_back = lax.optimization_barrier((mine, w_back))
        inputs += [mine, shift_send(mine, "sub", 1)]
    hidden, cot, grad_qk, grad_vo, back_keep, back_send = attend(
        inputs, pe, table, w_rows, w_out, w_back, owners, heads
    )
    hidden, cot, grad_qk, grad_vo = [hidden], [cot], [grad_qk], [grad_vo]

    back_blocks = join(back_keep, shift_send(back_send, "sub", 1))
    own_back = back_blocks[0]
    back_blocks = [own_back] + [
        shift_send(block, "tm", step + 1) for step, block in enumerate(back_blocks[1:])
    ]
    sums = []
    for lefts, grads in ((hidden + cot, grad_vo), (hidden, grad_qk)):
        if grads is grad_qk:
            grads, own_back = lax.optimization_barrier((grads, own_back))
        keep, side_blocks = weight_terms(grads, lefts, owners, sides)
        arrived = [shift_send(b, "rows", j + 1) for j, b in enumerate(side_blocks)]
        if grads is grad_vo:
            arrived, back_blocks[1] = lax.optimization_barrier((arrived, back_blocks[1]))
            arrived, back_blocks[2] = lax.optimization_barrier((arrived, back_blocks[2]))
            arrived, back_blocks[3] = lax.optimization_barrier((arrived, back_blocks[3]))
        own, blocks = combine(keep, arrived)
        sums.append([own] + [shift_send(b, "tm", step + 1) for step, b in enumerate(blocks)])
    grad_w_qkv, grad_w_out_t = finish(*sums)
    own_cot = lax.dynamic_slice_in_dim(cotangent, core * width, width, 2)
    return (place(back_blocks, own_cot), grad_w_qkv, grad_w_out_t)


def solution(mesh):
    return jax.shard_map(
        per_device,
        mesh=mesh,
        in_specs=(
            P("tm", ("req", "rows"), None),
            P("tm", ("req", "rows"), None),
            P(None, None, "sub"),
            P("sub", None),
            P(),
        ),
        out_specs=(
            P("tm", ("req", "rows"), "sub"),
            P(("req", "tm", "rows"), None, "sub"),
            P(("req", "tm", "rows"), "sub"),
        ),
        check_vma=False,
    )
```

```python
import functools
import math

import jax
import jax.numpy as jnp
from jax import lax
from jax.experimental import pallas as pl
from jax.experimental.pallas import tpu as pltpu
from jax.sharding import PartitionSpec as P

H = 8
VMEM = pl.BlockSpec(memory_space=pltpu.VMEM)
BF16 = jnp.bfloat16
F32 = jnp.float32


def params(limit=32 << 20):
    return pltpu.CompilerParams(vmem_limit_bytes=limit)


def shift_send(array, axis, step):
    size = lax.axis_size(axis)
    return lax.ppermute(array, axis, [(i, (i + step) % size) for i in range(size)])


def dot_nn(a, b):
    return lax.dot_general(a, b, (((1,), (0,)), ((), ())), preferred_element_type=F32)


def dot_nt(a, b):
    return lax.dot_general(a, b, (((1,), (1,)), ((), ())), preferred_element_type=F32)


def dot_tn(a, b):
    return lax.dot_general(a, b, (((0,), (0,)), ((), ())), preferred_element_type=F32)


def positional(frame_pos, channels):
    half = channels // 2
    frequency = jnp.exp(-math.log(10000.0) * jnp.arange(half, dtype=F32) * 2.0 / channels)
    angles = frame_pos.astype(F32)[:, None] * frequency[None, :]
    return jnp.concatenate((jnp.sin(angles), jnp.cos(angles)), axis=1)


def by_position(frames, width, back=False):
    rows = frames * width
    inner = width if back else frames
    outer = rows // inner
    row = lax.broadcasted_iota(jnp.int32, (rows, 1), 0)
    col = lax.broadcasted_iota(jnp.int32, (rows, rows), 1)
    source = lax.rem(row, inner) * outer + lax.div(row, inner)
    return jnp.where(col == source, 1.0, 0.0).astype(BF16)


def table_kernel(frames, owners, bias_ref, table_ref):
    heads, lanes = bias_ref.shape
    group = table_ref.shape[0]
    span = frames // owners
    me = lax.axis_index("tm")

    def place_of(index):
        return lax.rem(lax.div(index, span), group // frames)

    def frame_of(index):
        owner = lax.rem(me - lax.div(index, group // owners) + owners, owners)
        return owner * span + lax.rem(index, span)

    row = lax.broadcasted_iota(jnp.int32, (group, 1), 0)
    col = lax.broadcasted_iota(jnp.int32, (1, group), 1)
    same = place_of(row) == place_of(col)
    left = jnp.where(frame_of(row) == col, 1.0, 0.0)
    right = jnp.where(row == frame_of(col), 1.0, 0.0)

    def exact(a, b):
        return lax.dot_general(
            a, b, (((1,), (0,)), ((), ())), precision=lax.Precision.HIGHEST,
            preferred_element_type=F32,
        )

    for h in range(heads):
        spread = jnp.broadcast_to(bias_ref[h : h + 1, :], (group, lanes))
        skewed = pltpu.roll(spread, (1 - frames) % lanes, 1, stride=1, stride_axis=0)
        turned_bias = exact(left, exact(skewed[:, :group], right))
        table_ref[:, h * group : (h + 1) * group] = jnp.where(same, turned_bias, -1e30)


def send_blocks(latents, cotangent, count):
    width = latents.shape[1] // count
    me = lax.axis_index("tm")
    sent = jnp.where(lax.axis_index("sub") == 0, latents, cotangent)
    return [cut(sent, lax.rem(me + step, count), width) for step in range(1, count)]


def cut(array, owner, width):
    block = lax.dynamic_slice_in_dim(array, owner * width, width, 1)
    return jnp.swapaxes(block, 0, 1).reshape(-1, array.shape[2])


def bias_of_rows(time_bias, heads, frames, owners, group):
    own = lax.dynamic_slice_in_dim(time_bias, lax.axis_index("sub") * heads, heads, 0)
    lanes = -(-max(2 * frames - 1, group) // 128) * 128
    own = jnp.pad(own, ((0, 0), (0, lanes - own.shape[1])))
    return pl.pallas_call(
        functools.partial(table_kernel, frames, owners),
        out_shape=jax.ShapeDtypeStruct((group, heads * group), F32),
        in_specs=[VMEM],
        out_specs=VMEM,
        compiler_params=params(),
        name="bias_of_rows",
    )(own)


def attend_kernel(owners, heads, *refs):
    parts = 2 * owners
    inputs, refs = refs[:parts], refs[parts:]
    pe_ref, table_ref, w_qkv_ref, w_out_ref, w_own_ref, w_other_ref = refs[:6]
    hidden_ref, cot_ref, dqk_ref, dvo_ref, back_keep, back_send = refs[6:12]
    q_ref, k_ref, v_ref, g_ref = refs[12:]

    core = lax.axis_index("sub")
    rows, channels = hidden_ref.shape
    width = q_ref.shape[1]
    size = width // heads
    group = table_ref.shape[0]
    span = pe_ref.shape[0] // owners
    chunk = rows // owners
    piece = group // owners
    inv_root = 1.0 / math.sqrt(size)

    for step in range(owners):
        at = slice(step * chunk, (step + 1) * chunk)
        first, second = inputs[2 * step][...], inputs[2 * step + 1][...]
        if step == 0:
            lat, cot = first, second
        else:
            lat = jnp.where(core == 0, first, second)
            cot = jnp.where(core == 0, second, first)
        pe = pe_ref[step * span : (step + 1) * span, :]
        lat = lat.astype(F32).reshape(chunk // span, span, channels) + pe[None]
        hidden_ref[at, :] = lat.reshape(chunk, channels).astype(BF16)
        cot_ref[at, :] = cot

    hidden = hidden_ref[...]
    qkv = dot_nt(hidden, w_qkv_ref[...].reshape(3 * width, channels)).astype(BF16)
    for t, ref in enumerate((q_ref, k_ref, v_ref)):
        ref[...] = qkv[:, t * width : (t + 1) * width]
    g_ref[...] = dot_nt(cot_ref[...], w_out_ref[...]).astype(BF16)

    lane = lax.broadcasted_iota(jnp.int32, (group, width), 1)
    masks = [(lane >= h * size) & (lane < (h + 1) * size) for h in range(heads)]
    zero = jnp.zeros((group, width), BF16)

    def stack(value):
        return jnp.concatenate([jnp.where(mask, value, zero) for mask in masks], axis=0)

    def flip(value):
        return jnp.concatenate(
            [value[:, h * group : (h + 1) * group].T for h in range(heads)], axis=1
        )

    def rows_of(ref, start):
        return jnp.concatenate(
            [ref[k * chunk + start : k * chunk + start + piece, :] for k in range(owners)], axis=0
        )

    def put(ref, start, *halves):
        value = jnp.concatenate(halves, axis=1).astype(BF16)
        for k in range(owners):
            at = k * chunk + start
            ref[at : at + piece, :] = value[k * piece : (k + 1) * piece, :]

    starts = list(range(0, chunk, piece))
    wide = 2
    for some in [starts[i : i + wide] for i in range(0, len(starts), wide)]:
        rows = [[rows_of(ref, at) for ref in (q_ref, k_ref, v_ref, g_ref)] for at in some]
        queries, grads = [stack(r[0]) for r in rows], [stack(r[3]) for r in rows]
        scores = [dot_nt(r[1], q) * inv_root + table_ref[...] for r, q in zip(rows, queries)]
        grad_probs = [dot_nt(r[2], g) for r, g in zip(rows, grads)]
        raw = [jnp.exp(x - jnp.max(x, axis=0, keepdims=True)) for x in scores]
        probs = [x / jnp.sum(x, axis=0, keepdims=True) for x in raw]
        low = [p.astype(BF16) for p in probs]
        grad_value = [dot_nn(p, g) for p, g in zip(low, grads)]
        row_dot = [jnp.sum(p * u, axis=0, keepdims=True) for p, u in zip(probs, grad_probs)]
        grad_scores = [
            (p * (u - d) * inv_root).astype(BF16) for p, u, d in zip(probs, grad_probs, row_dot)
        ]
        attn_out = [dot_nn(flip(p), stack(r[2])) for p, r in zip(low, rows)]
        grad_key = [dot_nn(d, q) for d, q in zip(grad_scores, queries)]
        grad_query = [dot_nn(flip(d), stack(r[1])) for d, r in zip(grad_scores, rows)]
        for n, at in enumerate(some):
            put(dqk_ref, at, grad_query[n], grad_key[n])
            put(dvo_ref, at, grad_value[n], attn_out[n])

    grads = jnp.concatenate([dqk_ref[...], dvo_ref[:, :width]], axis=1)
    for w_ref, back_ref in ((w_own_ref, back_keep), (w_other_ref, back_send)):
        back = dot_nn(grads, w_ref[...]).astype(BF16)
        for k in range(owners):
            back_ref[(owners - k) % owners] = back[k * chunk : (k + 1) * chunk, :]


def attend(inputs, pe, table, w_qkv, w_out, w_back, owners, heads):
    chunk, channels = inputs[0].shape
    rows = chunk * owners
    width = w_qkv.shape[1]
    outs = [
        jax.ShapeDtypeStruct((rows, channels), BF16),
        jax.ShapeDtypeStruct((rows, channels), BF16),
        jax.ShapeDtypeStruct((rows, 2 * width), BF16),
        jax.ShapeDtypeStruct((rows, 2 * width), BF16),
        jax.ShapeDtypeStruct((owners, chunk, width), BF16),
        jax.ShapeDtypeStruct((owners, chunk, width), BF16),
    ]
    return pl.pallas_call(
        functools.partial(attend_kernel, owners, heads),
        out_shape=outs,
        in_specs=[VMEM] * (len(inputs) + 6),
        out_specs=[VMEM] * len(outs),
        scratch_shapes=[pltpu.VMEM((rows, width), BF16)] * 4,
        compiler_params=params(),
        name="attend",
    )(*inputs, pe, table, w_qkv, w_out, *w_back)


def weight_kernel(owners, sides, block, parts, count, *refs):
    grads, lefts, outs = refs[:parts], refs[parts : parts + count], refs[parts + count :]
    me, side = lax.axis_index("tm"), lax.axis_index("rows")
    values = [ref[...] for ref in grads]

    def product(lefts, columns):
        total = dot_tn(lefts[0][...], values[0][:, columns])
        for left, value in zip(lefts[1:], values[1:]):
            total = total + dot_tn(left[...], value[:, columns])
        return total

    columns = values[0].shape[1]
    if count > parts:
        low, high = columns // 2 // 128 * 128, -(-(columns // 2) // 128) * 128
        lower = product(lefts[:parts], slice(0, high))
        upper = product(lefts[parts:], slice(low, columns))
        pieces = [lower[:, :low]]
        if high > low:
            lane = lax.broadcasted_iota(jnp.int32, (lower.shape[0], high - low), 1) + low
            shared = jnp.where(lane < columns // 2, lower[:, low:], upper[:, : high - low])
            pieces.append(shared)
        full = jnp.concatenate(pieces + [upper[:, high - low :]], axis=1)
    else:
        full = product(lefts, slice(0, columns))
    if block % 16:
        outs[0][...] = full
        return
    for z in range(owners):
        slot = lax.rem(z - me + owners, owners)
        rows = [full[(z * sides + x) * block :][:block] for x in range(sides)]
        for j in range(sides):
            turned = rows[j]
            for shift in range(1, sides):
                turned = jnp.where(side == shift, rows[(j + shift) % sides], turned)
            outs[j][slot] = turned if j == 0 else turned.astype(BF16)


def weight_terms(grads, lefts, owners, sides):
    channels, columns = lefts[0].shape[1], grads[0].shape[1]
    block = channels // (owners * sides)
    if block % 16 == 0:
        keep = jax.ShapeDtypeStruct((owners, block, columns), F32)
        outs = [keep] + [jax.ShapeDtypeStruct((owners, block, columns), BF16)] * (sides - 1)
    else:
        outs = [jax.ShapeDtypeStruct((channels, columns), F32)]
    result = pl.pallas_call(
        functools.partial(weight_kernel, owners, sides, block, len(grads), len(lefts)),
        out_shape=outs,
        in_specs=[VMEM] * (len(grads) + len(lefts)),
        out_specs=[VMEM] * len(outs),
        compiler_params=params(),
        name="weight_terms",
    )(*grads, *lefts)
    if block % 16 == 0:
        return result[0], list(result[1:])
    full = result[0].reshape(owners, sides, block, columns)
    full = jnp.roll(full, (-lax.axis_index("tm"), -lax.axis_index("rows")), (0, 1))
    return full[:, 0], [full[:, j].astype(BF16) for j in range(1, sides)]


def combine_kernel(keep_ref, *refs):
    owners = keep_ref.shape[0]
    arrived, outs = refs[: len(refs) - owners], refs[len(refs) - owners :]
    for slot in range(owners):
        total = keep_ref[slot]
        for ref in arrived:
            total = total + ref[slot].astype(F32)
        outs[slot][...] = total.astype(outs[slot].dtype)


def combine(keep, arrived):
    owners = keep.shape[0]
    outs = [jax.ShapeDtypeStruct(keep.shape[1:], F32)]
    outs += [jax.ShapeDtypeStruct(keep.shape[1:], BF16)] * (owners - 1)
    result = pl.pallas_call(
        combine_kernel,
        out_shape=outs,
        in_specs=[VMEM] * (1 + len(arrived)),
        out_specs=[VMEM] * owners,
        compiler_params=params(),
        name="combine",
    )(keep, *arrived)
    return result[0], result[1:]


def join_kernel(keep_ref, arrived_ref, *outs):
    for slot, out in enumerate(outs):
        total = keep_ref[slot].astype(F32) + arrived_ref[slot].astype(F32)
        half = total.shape[0] // 2
        out[...] = jnp.concatenate([total[:half], total[half:]], axis=1).astype(BF16)


def join(keep, arrived):
    owners, rows, width = keep.shape
    return pl.pallas_call(
        join_kernel,
        out_shape=[jax.ShapeDtypeStruct((rows // 2, 2 * width), BF16)] * owners,
        in_specs=[VMEM] * 2,
        out_specs=[VMEM] * owners,
        compiler_params=params(),
        name="join",
    )(keep, arrived)


def finish_kernel(count, *refs):
    ins, (w_qkv_ref, w_out_ref) = refs[:-2], refs[-2:]

    def total(parts):
        value = parts[0][...]
        for ref in parts[1:]:
            value = value + ref[...].astype(F32)
        return value

    width = w_out_ref.shape[1]
    value_out, query_key = total(ins[:count]), total(ins[count:])
    w_qkv_ref[0] = query_key[:, :width]
    w_qkv_ref[1] = query_key[:, width:]
    w_qkv_ref[2] = value_out[:, :width]
    w_out_ref[...] = value_out[:, width:]


def finish(value_out, query_key):
    block, width = value_out[0].shape[0], value_out[0].shape[1] // 2
    count = len(value_out)
    w_qkv, w_out = pl.pallas_call(
        functools.partial(finish_kernel, count),
        out_shape=[
            jax.ShapeDtypeStruct((3, block, width), F32),
            jax.ShapeDtypeStruct((block, width), F32),
        ],
        in_specs=[VMEM] * (2 * count),
        out_specs=[VMEM] * 2,
        compiler_params=params(),
        name="finish",
    )(*value_out, *query_key)
    return jnp.transpose(w_qkv, (1, 0, 2)), w_out


def place_kernel(*refs):
    blocks, cot_ref, out_ref = refs[:-2], refs[-2], refs[-1]
    count = len(blocks)
    frames, positions, channels = out_ref.shape
    width = positions // count
    me = lax.axis_index("tm")
    order = by_position(frames, width, back=True)
    for step, ref in enumerate(blocks):
        start = pl.multiple_of(lax.rem(me - step + count, count) * width, width)
        rows = dot_nn(order, unfold(ref[...])).reshape(frames, width, channels)
        at = pl.ds(start, width)
        out_ref[:, at, :] = (cot_ref[:, at, :].astype(F32) + rows).astype(BF16)


def unfold(block):
    channels = block.shape[1] // 2
    return jnp.concatenate([block[:, :channels], block[:, channels:]], axis=0)


def place(blocks, cot):
    frames = cot.shape[0]
    count = len(blocks)
    chunk, channels = 2 * blocks[0].shape[0], blocks[0].shape[1] // 2
    width = chunk // frames
    if width % 16 == 0:
        return pl.pallas_call(
            place_kernel,
            out_shape=jax.ShapeDtypeStruct((frames, count * width, channels), BF16),
            in_specs=[VMEM] * (count + 1),
            out_specs=VMEM,
            compiler_params=params(),
            name="place",
        )(*blocks, cot)
    ordered = jnp.stack([unfold(b) for b in blocks[::-1]])
    ordered = jnp.roll(ordered, lax.axis_index("tm") + 1, 0)
    ordered = ordered.reshape(count, width, frames, channels)
    moved = jnp.transpose(ordered, (2, 0, 1, 3)).reshape(frames, count * width, channels)
    return (cot.astype(F32) + moved.astype(F32)).astype(BF16)


def per_device(latents, cotangent, w_qkv, w_out, time_bias):
    span, positions, channels = latents.shape
    owners, sides = lax.axis_size("tm"), lax.axis_size("rows")
    frames = span * owners
    heads = H // lax.axis_size("sub")
    group = max(frames, 128)
    me = lax.axis_index("tm")

    core = lax.axis_index("sub")
    width = w_qkv.shape[2]

    sends = send_blocks(latents, cotangent, owners)
    table = bias_of_rows(time_bias, heads, frames, owners, group)
    inputs = [cut(a, me, positions // owners) for a in (latents, cotangent)]
    owner = lax.rem(me - jnp.arange(owners, dtype=jnp.int32) + owners, owners)
    frame_pos = owner[:, None] * span + jnp.arange(span, dtype=jnp.int32)[None]
    pe = positional(frame_pos.reshape(-1), channels)
    w_rows = jnp.transpose(w_qkv, (1, 2, 0))
    w_flat = w_rows.reshape(3 * width, channels)
    w_back = [
        lax.dynamic_slice_in_dim(w_flat, which * width, width, 1) for which in (core, 1 - core)
    ]
    for step, block in enumerate(sends):
        mine = shift_send(block, "tm", step + 1)
        if step == 0:
            mine, w_back = lax.optimization_barrier((mine, w_back))
        inputs += [mine, shift_send(mine, "sub", 1)]
    hidden, cot, grad_qk, grad_vo, back_keep, back_send = attend(
        inputs, pe, table, w_rows, w_out, w_back, owners, heads
    )
    hidden, cot, grad_qk, grad_vo = [hidden], [cot], [grad_qk], [grad_vo]

    back_blocks = join(back_keep, shift_send(back_send, "sub", 1))
    own_back = back_blocks[0]
    back_blocks = [own_back] + [
        shift_send(block, "tm", step + 1) for step, block in enumerate(back_blocks[1:])
    ]
    sums = []
    for lefts, grads in ((hidden + cot, grad_vo), (hidden, grad_qk)):
        if grads is grad_qk:
            grads, own_back = lax.optimization_barrier((grads, own_back))
        keep, side_blocks = weight_terms(grads, lefts, owners, sides)
        arrived = [shift_send(b, "rows", j + 1) for j, b in enumerate(side_blocks)]
        if grads is grad_vo:
            arrived, back_blocks[1] = lax.optimization_barrier((arrived, back_blocks[1]))
            arrived, back_blocks[2] = lax.optimization_barrier((arrived, back_blocks[2]))
            arrived, back_blocks[3] = lax.optimization_barrier((arrived, back_blocks[3]))
        own, blocks = combine(keep, arrived)
        sums.append([own] + [shift_send(b, "tm", step + 1) for step, b in enumerate(blocks)])
    grad_w_qkv, grad_w_out_t = finish(*sums)
    own_cot = lax.dynamic_slice_in_dim(cotangent, core * width, width, 2)
    return (place(back_blocks, own_cot), grad_w_qkv, grad_w_out_t)


def solution(mesh):
    return jax.shard_map(
        per_device,
        mesh=mesh,
        in_specs=(
            P("tm", ("req", "rows"), None),
            P("tm", ("req", "rows"), None),
            P(None, None, "sub"),
            P("sub", None),
            P(),
        ),
        out_specs=(
            P("tm", ("req", "rows"), "sub"),
            P(("req", "tm", "rows"), None, "sub"),
            P(("req", "tm", "rows"), "sub"),
        ),
        check_vma=False,
    )
```

```python
import functools
import math

import jax
import jax.numpy as jnp
from jax import lax
from jax.experimental import pallas as pl
from jax.experimental.pallas import tpu as pltpu
from jax.sharding import PartitionSpec as P

H = 8
VMEM = pl.BlockSpec(memory_space=pltpu.VMEM)
BF16 = jnp.bfloat16
F32 = jnp.float32


def params(limit=32 << 20):
    return pltpu.CompilerParams(vmem_limit_bytes=limit)


def shift_send(array, axis, step):
    size = lax.axis_size(axis)
    return lax.ppermute(array, axis, [(i, (i + step) % size) for i in range(size)])


def dot_nn(a, b):
    return lax.dot_general(a, b, (((1,), (0,)), ((), ())), preferred_element_type=F32)


def dot_nt(a, b):
    return lax.dot_general(a, b, (((1,), (1,)), ((), ())), preferred_element_type=F32)


def dot_tn(a, b):
    return lax.dot_general(a, b, (((0,), (0,)), ((), ())), preferred_element_type=F32)


def positional(frame_pos, channels):
    half = channels // 2
    frequency = jnp.exp(-math.log(10000.0) * jnp.arange(half, dtype=F32) * 2.0 / channels)
    angles = frame_pos.astype(F32)[:, None] * frequency[None, :]
    return jnp.concatenate((jnp.sin(angles), jnp.cos(angles)), axis=1)


def by_position(frames, width, back=False):
    rows = frames * width
    inner = width if back else frames
    outer = rows // inner
    row = lax.broadcasted_iota(jnp.int32, (rows, 1), 0)
    col = lax.broadcasted_iota(jnp.int32, (rows, rows), 1)
    source = lax.rem(row, inner) * outer + lax.div(row, inner)
    return jnp.where(col == source, 1.0, 0.0).astype(BF16)


def table_kernel(frames, owners, bias_ref, table_ref):
    heads, lanes = bias_ref.shape
    group = table_ref.shape[0]
    span = frames // owners
    me = lax.axis_index("tm")

    def place_of(index):
        return lax.rem(lax.div(index, span), group // frames)

    def frame_of(index):
        owner = lax.rem(me - lax.div(index, group // owners) + owners, owners)
        return owner * span + lax.rem(index, span)

    row = lax.broadcasted_iota(jnp.int32, (group, 1), 0)
    col = lax.broadcasted_iota(jnp.int32, (1, group), 1)
    same = place_of(row) == place_of(col)
    left = jnp.where(frame_of(row) == col, 1.0, 0.0)
    right = jnp.where(row == frame_of(col), 1.0, 0.0)

    def exact(a, b):
        return lax.dot_general(
            a, b, (((1,), (0,)), ((), ())), precision=lax.Precision.HIGHEST,
            preferred_element_type=F32,
        )

    for h in range(heads):
        spread = jnp.broadcast_to(bias_ref[h : h + 1, :], (group, lanes))
        skewed = pltpu.roll(spread, (1 - frames) % lanes, 1, stride=1, stride_axis=0)
        turned_bias = exact(left, exact(skewed[:, :group], right))
        table_ref[:, h * group : (h + 1) * group] = jnp.where(same, turned_bias, -1e30)


def send_blocks(latents, cotangent, count):
    width = latents.shape[1] // count
    me = lax.axis_index("tm")
    sent = jnp.where(lax.axis_index("sub") == 0, latents, cotangent)
    return [cut(sent, lax.rem(me + step, count), width) for step in range(1, count)]


def cut(array, owner, width):
    block = lax.dynamic_slice_in_dim(array, owner * width, width, 1)
    return jnp.swapaxes(block, 0, 1).reshape(-1, array.shape[2])


def bias_of_rows(time_bias, heads, frames, owners, group):
    own = lax.dynamic_slice_in_dim(time_bias, lax.axis_index("sub") * heads, heads, 0)
    lanes = -(-max(2 * frames - 1, group) // 128) * 128
    own = jnp.pad(own, ((0, 0), (0, lanes - own.shape[1])))
    return pl.pallas_call(
        functools.partial(table_kernel, frames, owners),
        out_shape=jax.ShapeDtypeStruct((group, heads * group), F32),
        in_specs=[VMEM],
        out_specs=VMEM,
        compiler_params=params(),
        name="bias_of_rows",
    )(own)


def attend_kernel(owners, heads, *refs):
    parts = 2 * owners
    inputs, refs = refs[:parts], refs[parts:]
    pe_ref, table_ref, w_qkv_ref, w_out_ref, w_own_ref, w_other_ref = refs[:6]
    hidden_ref, cot_ref, dqk_ref, dvo_ref, back_keep, back_send = refs[6:12]
    q_ref, k_ref, v_ref, g_ref = refs[12:]

    core = lax.axis_index("sub")
    rows, channels = hidden_ref.shape
    width = q_ref.shape[1]
    size = width // heads
    group = table_ref.shape[0]
    span = pe_ref.shape[0] // owners
    chunk = rows // owners
    piece = group // owners
    inv_root = 1.0 / math.sqrt(size)

    for step in range(owners):
        at = slice(step * chunk, (step + 1) * chunk)
        first, second = inputs[2 * step][...], inputs[2 * step + 1][...]
        if step == 0:
            lat, cot = first, second
        else:
            lat = jnp.where(core == 0, first, second)
            cot = jnp.where(core == 0, second, first)
        pe = pe_ref[step * span : (step + 1) * span, :]
        lat = lat.astype(F32).reshape(chunk // span, span, channels) + pe[None]
        hidden_ref[at, :] = lat.reshape(chunk, channels).astype(BF16)
        cot_ref[at, :] = cot

    hidden = hidden_ref[...]
    qkv = dot_nt(hidden, w_qkv_ref[...].reshape(3 * width, channels)).astype(BF16)
    for t, ref in enumerate((q_ref, k_ref, v_ref)):
        ref[...] = qkv[:, t * width : (t + 1) * width]
    g_ref[...] = dot_nt(cot_ref[...], w_out_ref[...]).astype(BF16)

    lane = lax.broadcasted_iota(jnp.int32, (group, width), 1)
    masks = [(lane >= h * size) & (lane < (h + 1) * size) for h in range(heads)]
    zero = jnp.zeros((group, width), BF16)

    def stack(value):
        return jnp.concatenate([jnp.where(mask, value, zero) for mask in masks], axis=0)

    def flip(value):
        return jnp.concatenate(
            [value[:, h * group : (h + 1) * group].T for h in range(heads)], axis=1
        )

    def rows_of(ref, start):
        return jnp.concatenate(
            [ref[k * chunk + start : k * chunk + start + piece, :] for k in range(owners)], axis=0
        )

    def put(ref, start, *halves):
        value = jnp.concatenate(halves, axis=1).astype(BF16)
        for k in range(owners):
            at = k * chunk + start
            ref[at : at + piece, :] = value[k * piece : (k + 1) * piece, :]

    starts = list(range(0, chunk, piece))
    wide = 2
    for some in [starts[i : i + wide] for i in range(0, len(starts), wide)]:
        rows = [[rows_of(ref, at) for ref in (q_ref, k_ref, v_ref, g_ref)] for at in some]
        queries, grads = [stack(r[0]) for r in rows], [stack(r[3]) for r in rows]
        scores = [dot_nt(r[1], q) * inv_root + table_ref[...] for r, q in zip(rows, queries)]
        grad_probs = [dot_nt(r[2], g) for r, g in zip(rows, grads)]
        raw = [jnp.exp(x - jnp.max(x, axis=0, keepdims=True)) for x in scores]
        probs = [x / jnp.sum(x, axis=0, keepdims=True) for x in raw]
        low = [p.astype(BF16) for p in probs]
        grad_value = [dot_nn(p, g) for p, g in zip(low, grads)]
        row_dot = [jnp.sum(p * u, axis=0, keepdims=True) for p, u in zip(probs, grad_probs)]
        grad_scores = [
            (p * (u - d) * inv_root).astype(BF16) for p, u, d in zip(probs, grad_probs, row_dot)
        ]
        attn_out = [dot_nn(flip(p), stack(r[2])) for p, r in zip(low, rows)]
        grad_key = [dot_nn(d, q) for d, q in zip(grad_scores, queries)]
        grad_query = [dot_nn(flip(d), stack(r[1])) for d, r in zip(grad_scores, rows)]
        for n, at in enumerate(some):
            put(dqk_ref, at, grad_query[n], grad_key[n])
            put(dvo_ref, at, grad_value[n], attn_out[n])

    grads = jnp.concatenate([dqk_ref[...], dvo_ref[:, :width]], axis=1)
    for w_ref, back_ref in ((w_own_ref, back_keep), (w_other_ref, back_send)):
        back = dot_nn(grads, w_ref[...]).astype(BF16)
        for k in range(owners):
            back_ref[(owners - k) % owners] = back[k * chunk : (k + 1) * chunk, :]


def attend(inputs, pe, table, w_qkv, w_out, w_back, owners, heads):
    chunk, channels = inputs[0].shape
    rows = chunk * owners
    width = w_qkv.shape[1]
    outs = [
        jax.ShapeDtypeStruct((rows, channels), BF16),
        jax.ShapeDtypeStruct((rows, channels), BF16),
        jax.ShapeDtypeStruct((rows, 2 * width), BF16),
        jax.ShapeDtypeStruct((rows, 2 * width), BF16),
        jax.ShapeDtypeStruct((owners, chunk, width), BF16),
        jax.ShapeDtypeStruct((owners, chunk, width), BF16),
    ]
    return pl.pallas_call(
        functools.partial(attend_kernel, owners, heads),
        out_shape=outs,
        in_specs=[VMEM] * (len(inputs) + 6),
        out_specs=[VMEM] * len(outs),
        scratch_shapes=[pltpu.VMEM((rows, width), BF16)] * 4,
        compiler_params=params(),
        name="attend",
    )(*inputs, pe, table, w_qkv, w_out, *w_back)


def weight_kernel(owners, sides, block, parts, count, *refs):
    grads, lefts, outs = refs[:parts], refs[parts : parts + count], refs[parts + count :]
    me, side = lax.axis_index("tm"), lax.axis_index("rows")
    values = [ref[...] for ref in grads]

    def product(lefts, columns):
        total = dot_tn(lefts[0][...], values[0][:, columns])
        for left, value in zip(lefts[1:], values[1:]):
            total = total + dot_tn(left[...], value[:, columns])
        return total

    columns = values[0].shape[1]
    if count > parts:
        low, high = columns // 2 // 128 * 128, -(-(columns // 2) // 128) * 128
        lower = product(lefts[:parts], slice(0, high))
        upper = product(lefts[parts:], slice(low, columns))
        pieces = [lower[:, :low]]
        if high > low:
            lane = lax.broadcasted_iota(jnp.int32, (lower.shape[0], high - low), 1) + low
            shared = jnp.where(lane < columns // 2, lower[:, low:], upper[:, : high - low])
            pieces.append(shared)
        full = jnp.concatenate(pieces + [upper[:, high - low :]], axis=1)
    else:
        full = product(lefts, slice(0, columns))
    if block % 16:
        outs[0][...] = full
        return
    for z in range(owners):
        slot = lax.rem(z - me + owners, owners)
        rows = [full[(z * sides + x) * block :][:block] for x in range(sides)]
        for j in range(sides):
            turned = rows[j]
            for shift in range(1, sides):
                turned = jnp.where(side == shift, rows[(j + shift) % sides], turned)
            outs[j][slot] = turned if j == 0 else turned.astype(BF16)


def weight_terms(grads, lefts, owners, sides):
    channels, columns = lefts[0].shape[1], grads[0].shape[1]
    block = channels // (owners * sides)
    if block % 16 == 0:
        keep = jax.ShapeDtypeStruct((owners, block, columns), F32)
        outs = [keep] + [jax.ShapeDtypeStruct((owners, block, columns), BF16)] * (sides - 1)
    else:
        outs = [jax.ShapeDtypeStruct((channels, columns), F32)]
    result = pl.pallas_call(
        functools.partial(weight_kernel, owners, sides, block, len(grads), len(lefts)),
        out_shape=outs,
        in_specs=[VMEM] * (len(grads) + len(lefts)),
        out_specs=[VMEM] * len(outs),
        compiler_params=params(),
        name="weight_terms",
    )(*grads, *lefts)
    if block % 16 == 0:
        return result[0], list(result[1:])
    full = result[0].reshape(owners, sides, block, columns)
    full = jnp.roll(full, (-lax.axis_index("tm"), -lax.axis_index("rows")), (0, 1))
    return full[:, 0], [full[:, j].astype(BF16) for j in range(1, sides)]


def combine_kernel(keep_ref, *refs):
    owners = keep_ref.shape[0]
    arrived, outs = refs[: len(refs) - owners], refs[len(refs) - owners :]
    for slot in range(owners):
        total = keep_ref[slot]
        for ref in arrived:
            total = total + ref[slot].astype(F32)
        outs[slot][...] = total.astype(outs[slot].dtype)


def combine(keep, arrived):
    owners = keep.shape[0]
    outs = [jax.ShapeDtypeStruct(keep.shape[1:], F32)]
    outs += [jax.ShapeDtypeStruct(keep.shape[1:], BF16)] * (owners - 1)
    result = pl.pallas_call(
        combine_kernel,
        out_shape=outs,
        in_specs=[VMEM] * (1 + len(arrived)),
        out_specs=[VMEM] * owners,
        compiler_params=params(),
        name="combine",
    )(keep, *arrived)
    return result[0], result[1:]


def join_kernel(keep_ref, arrived_ref, *outs):
    for slot, out in enumerate(outs):
        total = keep_ref[slot].astype(F32) + arrived_ref[slot].astype(F32)
        half = total.shape[0] // 2
        out[...] = jnp.concatenate([total[:half], total[half:]], axis=1).astype(BF16)


def join(keep, arrived):
    owners, rows, width = keep.shape
    return pl.pallas_call(
        join_kernel,
        out_shape=[jax.ShapeDtypeStruct((rows // 2, 2 * width), BF16)] * owners,
        in_specs=[VMEM] * 2,
        out_specs=[VMEM] * owners,
        compiler_params=params(),
        name="join",
    )(keep, arrived)


def finish_kernel(count, *refs):
    ins, (w_qkv_ref, w_out_ref) = refs[:-2], refs[-2:]

    def total(parts):
        value = parts[0][...]
        for ref in parts[1:]:
            value = value + ref[...].astype(F32)
        return value

    width = w_out_ref.shape[1]
    value_out, query_key = total(ins[:count]), total(ins[count:])
    w_qkv_ref[0] = query_key[:, :width]
    w_qkv_ref[1] = query_key[:, width:]
    w_qkv_ref[2] = value_out[:, :width]
    w_out_ref[...] = value_out[:, width:]


def finish(value_out, query_key):
    block, width = value_out[0].shape[0], value_out[0].shape[1] // 2
    count = len(value_out)
    w_qkv, w_out = pl.pallas_call(
        functools.partial(finish_kernel, count),
        out_shape=[
            jax.ShapeDtypeStruct((3, block, width), F32),
            jax.ShapeDtypeStruct((block, width), F32),
        ],
        in_specs=[VMEM] * (2 * count),
        out_specs=[VMEM] * 2,
        compiler_params=params(),
        name="finish",
    )(*value_out, *query_key)
    return jnp.transpose(w_qkv, (1, 0, 2)), w_out


def place_kernel(*refs):
    blocks, cot_ref, out_ref = refs[:-2], refs[-2], refs[-1]
    count = len(blocks)
    frames, positions, channels = out_ref.shape
    width = positions // count
    me = lax.axis_index("tm")
    order = by_position(frames, width, back=True)
    for step, ref in enumerate(blocks):
        start = pl.multiple_of(lax.rem(me - step + count, count) * width, width)
        rows = dot_nn(order, unfold(ref[...])).reshape(frames, width, channels)
        at = pl.ds(start, width)
        out_ref[:, at, :] = (cot_ref[:, at, :].astype(F32) + rows).astype(BF16)


def unfold(block):
    channels = block.shape[1] // 2
    return jnp.concatenate([block[:, :channels], block[:, channels:]], axis=0)


def place(blocks, cot):
    frames = cot.shape[0]
    count = len(blocks)
    chunk, channels = 2 * blocks[0].shape[0], blocks[0].shape[1] // 2
    width = chunk // frames
    if width % 16 == 0:
        return pl.pallas_call(
            place_kernel,
            out_shape=jax.ShapeDtypeStruct((frames, count * width, channels), BF16),
            in_specs=[VMEM] * (count + 1),
            out_specs=VMEM,
            compiler_params=params(),
            name="place",
        )(*blocks, cot)
    ordered = jnp.stack([unfold(b) for b in blocks[::-1]])
    ordered = jnp.roll(ordered, lax.axis_index("tm") + 1, 0)
    ordered = ordered.reshape(count, width, frames, channels)
    moved = jnp.transpose(ordered, (2, 0, 1, 3)).reshape(frames, count * width, channels)
    return (cot.astype(F32) + moved.astype(F32)).astype(BF16)


def per_device(latents, cotangent, w_qkv, w_out, time_bias):
    span, positions, channels = latents.shape
    owners, sides = lax.axis_size("tm"), lax.axis_size("rows")
    frames = span * owners
    heads = H // lax.axis_size("sub")
    group = max(frames, 128)
    me = lax.axis_index("tm")

    core = lax.axis_index("sub")
    width = w_qkv.shape[2]

    sends = send_blocks(latents, cotangent, owners)
    table = bias_of_rows(time_bias, heads, frames, owners, group)
    inputs = [cut(a, me, positions // owners) for a in (latents, cotangent)]
    owner = lax.rem(me - jnp.arange(owners, dtype=jnp.int32) + owners, owners)
    frame_pos = owner[:, None] * span + jnp.arange(span, dtype=jnp.int32)[None]
    pe = positional(frame_pos.reshape(-1), channels)
    w_rows = jnp.transpose(w_qkv, (1, 2, 0))
    w_flat = w_rows.reshape(3 * width, channels)
    w_back = [
        lax.dynamic_slice_in_dim(w_flat, which * width, width, 1) for which in (core, 1 - core)
    ]
    for step, block in enumerate(sends):
        mine = shift_send(block, "tm", step + 1)
        if step == 0:
            mine, w_back, table, inputs, pe = lax.optimization_barrier((mine, w_back, table, inputs, pe))
        inputs += [mine, shift_send(mine, "sub", 1)]
    hidden, cot, grad_qk, grad_vo, back_keep, back_send = attend(
        inputs, pe, table, w_rows, w_out, w_back, owners, heads
    )
    hidden, cot, grad_qk, grad_vo = [hidden], [cot], [grad_qk], [grad_vo]

    back_blocks = join(back_keep, shift_send(back_send, "sub", 1))
    own_back = back_blocks[0]
    back_blocks = [own_back] + [
        shift_send(block, "tm", step + 1) for step, block in enumerate(back_blocks[1:])
    ]
    sums = []
    for lefts, grads in ((hidden + cot, grad_vo), (hidden, grad_qk)):
        if grads is grad_qk:
            grads, own_back = lax.optimization_barrier((grads, own_back))
        keep, side_blocks = weight_terms(grads, lefts, owners, sides)
        arrived = [shift_send(b, "rows", j + 1) for j, b in enumerate(side_blocks)]
        if grads is grad_vo:
            arrived, back_blocks[1] = lax.optimization_barrier((arrived, back_blocks[1]))
            arrived, back_blocks[2] = lax.optimization_barrier((arrived, back_blocks[2]))
            arrived, back_blocks[3] = lax.optimization_barrier((arrived, back_blocks[3]))
        own, blocks = combine(keep, arrived)
        sums.append([own] + [shift_send(b, "tm", step + 1) for step, b in enumerate(blocks)])
    grad_w_qkv, grad_w_out_t = finish(*sums)
    own_cot = lax.dynamic_slice_in_dim(cotangent, core * width, width, 2)
    return (place(back_blocks, own_cot), grad_w_qkv, grad_w_out_t)


def solution(mesh):
    return jax.shard_map(
        per_device,
        mesh=mesh,
        in_specs=(
            P("tm", ("req", "rows"), None),
            P("tm", ("req", "rows"), None),
            P(None, None, "sub"),
            P("sub", None),
            P(),
        ),
        out_specs=(
            P("tm", ("req", "rows"), "sub"),
            P(("req", "tm", "rows"), None, "sub"),
            P(("req", "tm", "rows"), "sub"),
        ),
        check_vma=False,
    )
```

```python
import functools
import math

import jax
import jax.numpy as jnp
from jax import lax
from jax.experimental import pallas as pl
from jax.experimental.pallas import tpu as pltpu
from jax.sharding import PartitionSpec as P

H = 8
VMEM = pl.BlockSpec(memory_space=pltpu.VMEM)
BF16 = jnp.bfloat16
F32 = jnp.float32


def params(limit=32 << 20):
    return pltpu.CompilerParams(vmem_limit_bytes=limit)


def shift_send(array, axis, step):
    size = lax.axis_size(axis)
    return lax.ppermute(array, axis, [(i, (i + step) % size) for i in range(size)])


def dot_nn(a, b):
    return lax.dot_general(a, b, (((1,), (0,)), ((), ())), preferred_element_type=F32)


def dot_nt(a, b):
    return lax.dot_general(a, b, (((1,), (1,)), ((), ())), preferred_element_type=F32)


def dot_tn(a, b):
    return lax.dot_general(a, b, (((0,), (0,)), ((), ())), preferred_element_type=F32)


def positional(frame_pos, channels):
    half = channels // 2
    frequency = jnp.exp(-math.log(10000.0) * jnp.arange(half, dtype=F32) * 2.0 / channels)
    angles = frame_pos.astype(F32)[:, None] * frequency[None, :]
    return jnp.concatenate((jnp.sin(angles), jnp.cos(angles)), axis=1)


def by_position(frames, width, back=False):
    rows = frames * width
    inner = width if back else frames
    outer = rows // inner
    row = lax.broadcasted_iota(jnp.int32, (rows, 1), 0)
    col = lax.broadcasted_iota(jnp.int32, (rows, rows), 1)
    source = lax.rem(row, inner) * outer + lax.div(row, inner)
    return jnp.where(col == source, 1.0, 0.0).astype(BF16)


def table_kernel(frames, owners, bias_ref, table_ref):
    heads, lanes = bias_ref.shape
    group = table_ref.shape[0]
    span = frames // owners
    me = lax.axis_index("tm")

    def place_of(index):
        return lax.rem(lax.div(index, span), group // frames)

    def frame_of(index):
        owner = lax.rem(me - lax.div(index, group // owners) + owners, owners)
        return owner * span + lax.rem(index, span)

    row = lax.broadcasted_iota(jnp.int32, (group, 1), 0)
    col = lax.broadcasted_iota(jnp.int32, (1, group), 1)
    same = place_of(row) == place_of(col)
    left = jnp.where(frame_of(row) == col, 1.0, 0.0)
    right = jnp.where(row == frame_of(col), 1.0, 0.0)

    def exact(a, b):
        return lax.dot_general(
            a, b, (((1,), (0,)), ((), ())), precision=lax.Precision.HIGHEST,
            preferred_element_type=F32,
        )

    for h in range(heads):
        spread = jnp.broadcast_to(bias_ref[h : h + 1, :], (group, lanes))
        skewed = pltpu.roll(spread, (1 - frames) % lanes, 1, stride=1, stride_axis=0)
        turned_bias = exact(left, exact(skewed[:, :group], right))
        table_ref[:, h * group : (h + 1) * group] = jnp.where(same, turned_bias, -1e30)


def send_blocks(latents, cotangent, count):
    width = latents.shape[1] // count
    me = lax.axis_index("tm")
    sent = jnp.where(lax.axis_index("sub") == 0, latents, cotangent)
    return [cut(sent, lax.rem(me + step, count), width) for step in range(1, count)]


def cut(array, owner, width):
    block = lax.dynamic_slice_in_dim(array, owner * width, width, 1)
    return jnp.swapaxes(block, 0, 1).reshape(-1, array.shape[2])


def bias_of_rows(time_bias, heads, frames, owners, group):
    own = lax.dynamic_slice_in_dim(time_bias, lax.axis_index("sub") * heads, heads, 0)
    lanes = -(-max(2 * frames - 1, group) // 128) * 128
    own = jnp.pad(own, ((0, 0), (0, lanes - own.shape[1])))
    return pl.pallas_call(
        functools.partial(table_kernel, frames, owners),
        out_shape=jax.ShapeDtypeStruct((group, heads * group), F32),
        in_specs=[VMEM],
        out_specs=VMEM,
        compiler_params=params(),
        name="bias_of_rows",
    )(own)


def attend_kernel(owners, heads, *refs):
    parts = 2 * owners
    inputs, refs = refs[:parts], refs[parts:]
    pe_ref, table_ref, w_qkv_ref, w_out_ref, w_own_ref, w_other_ref = refs[:6]
    hidden_ref, cot_ref, dqk_ref, dvo_ref, back_keep, back_send = refs[6:12]
    q_ref, k_ref, v_ref, g_ref = refs[12:]

    core = lax.axis_index("sub")
    rows, channels = hidden_ref.shape
    width = q_ref.shape[1]
    size = width // heads
    group = table_ref.shape[0]
    span = pe_ref.shape[0] // owners
    chunk = rows // owners
    piece = group // owners
    inv_root = 1.0 / math.sqrt(size)

    for step in range(owners):
        at = slice(step * chunk, (step + 1) * chunk)
        first, second = inputs[2 * step][...], inputs[2 * step + 1][...]
        if step == 0:
            lat, cot = first, second
        else:
            lat = jnp.where(core == 0, first, second)
            cot = jnp.where(core == 0, second, first)
        pe = pe_ref[step * span : (step + 1) * span, :]
        lat = lat.astype(F32).reshape(chunk // span, span, channels) + pe[None]
        hidden_ref[at, :] = lat.reshape(chunk, channels).astype(BF16)
        cot_ref[at, :] = cot

    hidden = hidden_ref[...]
    qkv = dot_nt(hidden, w_qkv_ref[...].reshape(3 * width, channels)).astype(BF16)
    for t, ref in enumerate((q_ref, k_ref, v_ref)):
        ref[...] = qkv[:, t * width : (t + 1) * width]
    g_ref[...] = dot_nt(cot_ref[...], w_out_ref[...]).astype(BF16)

    lane = lax.broadcasted_iota(jnp.int32, (group, width), 1)
    masks = [(lane >= h * size) & (lane < (h + 1) * size) for h in range(heads)]
    zero = jnp.zeros((group, width), BF16)

    def stack(value):
        return jnp.concatenate([jnp.where(mask, value, zero) for mask in masks], axis=0)

    def flip(value):
        return jnp.concatenate(
            [value[:, h * group : (h + 1) * group].T for h in range(heads)], axis=1
        )

    def rows_of(ref, start):
        return jnp.concatenate(
            [ref[k * chunk + start : k * chunk + start + piece, :] for k in range(owners)], axis=0
        )

    def put(ref, start, *halves):
        value = jnp.concatenate(halves, axis=1).astype(BF16)
        for k in range(owners):
            at = k * chunk + start
            ref[at : at + piece, :] = value[k * piece : (k + 1) * piece, :]

    starts = list(range(0, chunk, piece))
    wide = 4
    for some in [starts[i : i + wide] for i in range(0, len(starts), wide)]:
        rows = [[rows_of(ref, at) for ref in (q_ref, k_ref, v_ref, g_ref)] for at in some]
        queries, grads = [stack(r[0]) for r in rows], [stack(r[3]) for r in rows]
        scores = [dot_nt(r[1], q) * inv_root + table_ref[...] for r, q in zip(rows, queries)]
        grad_probs = [dot_nt(r[2], g) for r, g in zip(rows, grads)]
        raw = [jnp.exp(x - jnp.max(x, axis=0, keepdims=True)) for x in scores]
        probs = [x / jnp.sum(x, axis=0, keepdims=True) for x in raw]
        low = [p.astype(BF16) for p in probs]
        grad_value = [dot_nn(p, g) for p, g in zip(low, grads)]
        row_dot = [jnp.sum(p * u, axis=0, keepdims=True) for p, u in zip(probs, grad_probs)]
        grad_scores = [
            (p * (u - d) * inv_root).astype(BF16) for p, u, d in zip(probs, grad_probs, row_dot)
        ]
        attn_out = [dot_nn(flip(p), stack(r[2])) for p, r in zip(low, rows)]
        grad_key = [dot_nn(d, q) for d, q in zip(grad_scores, queries)]
        grad_query = [dot_nn(flip(d), stack(r[1])) for d, r in zip(grad_scores, rows)]
        for n, at in enumerate(some):
            put(dqk_ref, at, grad_query[n], grad_key[n])
            put(dvo_ref, at, grad_value[n], attn_out[n])

    grads = jnp.concatenate([dqk_ref[...], dvo_ref[:, :width]], axis=1)
    for w_ref, back_ref in ((w_own_ref, back_keep), (w_other_ref, back_send)):
        back = dot_nn(grads, w_ref[...]).astype(BF16)
        for k in range(owners):
            back_ref[(owners - k) % owners] = back[k * chunk : (k + 1) * chunk, :]


def attend(inputs, pe, table, w_qkv, w_out, w_back, owners, heads):
    chunk, channels = inputs[0].shape
    rows = chunk * owners
    width = w_qkv.shape[1]
    outs = [
        jax.ShapeDtypeStruct((rows, channels), BF16),
        jax.ShapeDtypeStruct((rows, channels), BF16),
        jax.ShapeDtypeStruct((rows, 2 * width), BF16),
        jax.ShapeDtypeStruct((rows, 2 * width), BF16),
        jax.ShapeDtypeStruct((owners, chunk, width), BF16),
        jax.ShapeDtypeStruct((owners, chunk, width), BF16),
    ]
    return pl.pallas_call(
        functools.partial(attend_kernel, owners, heads),
        out_shape=outs,
        in_specs=[VMEM] * (len(inputs) + 6),
        out_specs=[VMEM] * len(outs),
        scratch_shapes=[pltpu.VMEM((rows, width), BF16)] * 4,
        compiler_params=params(),
        name="attend",
    )(*inputs, pe, table, w_qkv, w_out, *w_back)


def weight_kernel(owners, sides, block, parts, count, *refs):
    grads, lefts, outs = refs[:parts], refs[parts : parts + count], refs[parts + count :]
    me, side = lax.axis_index("tm"), lax.axis_index("rows")
    values = [ref[...] for ref in grads]

    def product(lefts, columns):
        total = dot_tn(lefts[0][...], values[0][:, columns])
        for left, value in zip(lefts[1:], values[1:]):
            total = total + dot_tn(left[...], value[:, columns])
        return total

    columns = values[0].shape[1]
    if count > parts:
        low, high = columns // 2 // 128 * 128, -(-(columns // 2) // 128) * 128
        lower = product(lefts[:parts], slice(0, high))
        upper = product(lefts[parts:], slice(low, columns))
        pieces = [lower[:, :low]]
        if high > low:
            lane = lax.broadcasted_iota(jnp.int32, (lower.shape[0], high - low), 1) + low
            shared = jnp.where(lane < columns // 2, lower[:, low:], upper[:, : high - low])
            pieces.append(shared)
        full = jnp.concatenate(pieces + [upper[:, high - low :]], axis=1)
    else:
        full = product(lefts, slice(0, columns))
    if block % 16:
        outs[0][...] = full
        return
    for z in range(owners):
        slot = lax.rem(z - me + owners, owners)
        rows = [full[(z * sides + x) * block :][:block] for x in range(sides)]
        for j in range(sides):
            turned = rows[j]
            for shift in range(1, sides):
                turned = jnp.where(side == shift, rows[(j + shift) % sides], turned)
            outs[j][slot] = turned if j == 0 else turned.astype(BF16)


def weight_terms(grads, lefts, owners, sides):
    channels, columns = lefts[0].shape[1], grads[0].shape[1]
    block = channels // (owners * sides)
    if block % 16 == 0:
        keep = jax.ShapeDtypeStruct((owners, block, columns), F32)
        outs = [keep] + [jax.ShapeDtypeStruct((owners, block, columns), BF16)] * (sides - 1)
    else:
        outs = [jax.ShapeDtypeStruct((channels, columns), F32)]
    result = pl.pallas_call(
        functools.partial(weight_kernel, owners, sides, block, len(grads), len(lefts)),
        out_shape=outs,
        in_specs=[VMEM] * (len(grads) + len(lefts)),
        out_specs=[VMEM] * len(outs),
        compiler_params=params(),
        name="weight_terms",
    )(*grads, *lefts)
    if block % 16 == 0:
        return result[0], list(result[1:])
    full = result[0].reshape(owners, sides, block, columns)
    full = jnp.roll(full, (-lax.axis_index("tm"), -lax.axis_index("rows")), (0, 1))
    return full[:, 0], [full[:, j].astype(BF16) for j in range(1, sides)]


def combine_kernel(keep_ref, *refs):
    owners = keep_ref.shape[0]
    arrived, outs = refs[: len(refs) - owners], refs[len(refs) - owners :]
    for slot in range(owners):
        total = keep_ref[slot]
        for ref in arrived:
            total = total + ref[slot].astype(F32)
        outs[slot][...] = total.astype(outs[slot].dtype)


def combine(keep, arrived):
    owners = keep.shape[0]
    outs = [jax.ShapeDtypeStruct(keep.shape[1:], F32)]
    outs += [jax.ShapeDtypeStruct(keep.shape[1:], BF16)] * (owners - 1)
    result = pl.pallas_call(
        combine_kernel,
        out_shape=outs,
        in_specs=[VMEM] * (1 + len(arrived)),
        out_specs=[VMEM] * owners,
        compiler_params=params(),
        name="combine",
    )(keep, *arrived)
    return result[0], result[1:]


def join_kernel(keep_ref, arrived_ref, *outs):
    for slot, out in enumerate(outs):
        total = keep_ref[slot].astype(F32) + arrived_ref[slot].astype(F32)
        half = total.shape[0] // 2
        out[...] = jnp.concatenate([total[:half], total[half:]], axis=1).astype(BF16)


def join(keep, arrived):
    owners, rows, width = keep.shape
    return pl.pallas_call(
        join_kernel,
        out_shape=[jax.ShapeDtypeStruct((rows // 2, 2 * width), BF16)] * owners,
        in_specs=[VMEM] * 2,
        out_specs=[VMEM] * owners,
        compiler_params=params(),
        name="join",
    )(keep, arrived)


def finish_kernel(count, *refs):
    ins, (w_qkv_ref, w_out_ref) = refs[:-2], refs[-2:]

    def total(parts):
        value = parts[0][...]
        for ref in parts[1:]:
            value = value + ref[...].astype(F32)
        return value

    width = w_out_ref.shape[1]
    value_out, query_key = total(ins[:count]), total(ins[count:])
    w_qkv_ref[0] = query_key[:, :width]
    w_qkv_ref[1] = query_key[:, width:]
    w_qkv_ref[2] = value_out[:, :width]
    w_out_ref[...] = value_out[:, width:]


def finish(value_out, query_key):
    block, width = value_out[0].shape[0], value_out[0].shape[1] // 2
    count = len(value_out)
    w_qkv, w_out = pl.pallas_call(
        functools.partial(finish_kernel, count),
        out_shape=[
            jax.ShapeDtypeStruct((3, block, width), F32),
            jax.ShapeDtypeStruct((block, width), F32),
        ],
        in_specs=[VMEM] * (2 * count),
        out_specs=[VMEM] * 2,
        compiler_params=params(),
        name="finish",
    )(*value_out, *query_key)
    return jnp.transpose(w_qkv, (1, 0, 2)), w_out


def place_kernel(*refs):
    blocks, cot_ref, out_ref = refs[:-2], refs[-2], refs[-1]
    count = len(blocks)
    frames, positions, channels = out_ref.shape
    width = positions // count
    me = lax.axis_index("tm")
    order = by_position(frames, width, back=True)
    for step, ref in enumerate(blocks):
        start = pl.multiple_of(lax.rem(me - step + count, count) * width, width)
        rows = dot_nn(order, unfold(ref[...])).reshape(frames, width, channels)
        at = pl.ds(start, width)
        out_ref[:, at, :] = (cot_ref[:, at, :].astype(F32) + rows).astype(BF16)


def unfold(block):
    channels = block.shape[1] // 2
    return jnp.concatenate([block[:, :channels], block[:, channels:]], axis=0)


def place(blocks, cot):
    frames = cot.shape[0]
    count = len(blocks)
    chunk, channels = 2 * blocks[0].shape[0], blocks[0].shape[1] // 2
    width = chunk // frames
    if width % 16 == 0:
        return pl.pallas_call(
            place_kernel,
            out_shape=jax.ShapeDtypeStruct((frames, count * width, channels), BF16),
            in_specs=[VMEM] * (count + 1),
            out_specs=VMEM,
            compiler_params=params(),
            name="place",
        )(*blocks, cot)
    ordered = jnp.stack([unfold(b) for b in blocks[::-1]])
    ordered = jnp.roll(ordered, lax.axis_index("tm") + 1, 0)
    ordered = ordered.reshape(count, width, frames, channels)
    moved = jnp.transpose(ordered, (2, 0, 1, 3)).reshape(frames, count * width, channels)
    return (cot.astype(F32) + moved.astype(F32)).astype(BF16)


def per_device(latents, cotangent, w_qkv, w_out, time_bias):
    span, positions, channels = latents.shape
    owners, sides = lax.axis_size("tm"), lax.axis_size("rows")
    frames = span * owners
    heads = H // lax.axis_size("sub")
    group = max(frames, 128)
    me = lax.axis_index("tm")

    core = lax.axis_index("sub")
    width = w_qkv.shape[2]

    sends = send_blocks(latents, cotangent, owners)
    table = bias_of_rows(time_bias, heads, frames, owners, group)
    inputs = [cut(a, me, positions // owners) for a in (latents, cotangent)]
    owner = lax.rem(me - jnp.arange(owners, dtype=jnp.int32) + owners, owners)
    frame_pos = owner[:, None] * span + jnp.arange(span, dtype=jnp.int32)[None]
    pe = positional(frame_pos.reshape(-1), channels)
    w_rows = jnp.transpose(w_qkv, (1, 2, 0))
    w_flat = w_rows.reshape(3 * width, channels)
    w_back = [
        lax.dynamic_slice_in_dim(w_flat, which * width, width, 1) for which in (core, 1 - core)
    ]
    for step, block in enumerate(sends):
        mine = shift_send(block, "tm", step + 1)
        if step == 0:
            mine, w_back = lax.optimization_barrier((mine, w_back))
        inputs += [mine, shift_send(mine, "sub", 1)]
    hidden, cot, grad_qk, grad_vo, back_keep, back_send = attend(
        inputs, pe, table, w_rows, w_out, w_back, owners, heads
    )
    hidden, cot, grad_qk, grad_vo = [hidden], [cot], [grad_qk], [grad_vo]

    back_blocks = join(back_keep, shift_send(back_send, "sub", 1))
    own_back = back_blocks[0]
    back_blocks = [own_back] + [
        shift_send(block, "tm", step + 1) for step, block in enumerate(back_blocks[1:])
    ]
    sums = []
    for lefts, grads in ((hidden + cot, grad_vo), (hidden, grad_qk)):
        if grads is grad_qk:
            grads, own_back = lax.optimization_barrier((grads, own_back))
        keep, side_blocks = weight_terms(grads, lefts, owners, sides)
        arrived = [shift_send(b, "rows", j + 1) for j, b in enumerate(side_blocks)]
        if grads is grad_vo:
            arrived, back_blocks[1] = lax.optimization_barrier((arrived, back_blocks[1]))
            arrived, back_blocks[2] = lax.optimization_barrier((arrived, back_blocks[2]))
            arrived, back_blocks[3] = lax.optimization_barrier((arrived, back_blocks[3]))
        own, blocks = combine(keep, arrived)
        sums.append([own] + [shift_send(b, "tm", step + 1) for step, b in enumerate(blocks)])
    grad_w_qkv, grad_w_out_t = finish(*sums)
    own_cot = lax.dynamic_slice_in_dim(cotangent, core * width, width, 2)
    return (place(back_blocks, own_cot), grad_w_qkv, grad_w_out_t)


def solution(mesh):
    return jax.shard_map(
        per_device,
        mesh=mesh,
        in_specs=(
            P("tm", ("req", "rows"), None),
            P("tm", ("req", "rows"), None),
            P(None, None, "sub"),
            P("sub", None),
            P(),
        ),
        out_specs=(
            P("tm", ("req", "rows"), "sub"),
            P(("req", "tm", "rows"), None, "sub"),
            P(("req", "tm", "rows"), "sub"),
        ),
        check_vma=False,
    )
```
